32 devices in a mesh: tm: 8 (over z, y), head: 4 (over x, core).
Axes of the slice: x: 2, y: 2, z: 4, core: 2. Of those that a mesh axis runs over, the one named last changes fastest.
Arguments:
- queries: bfloat16 [2048, 3072], P('tm', 'head'), may hold values from -6 to 6
- key_input: bfloat16 [2048, 3072], P('tm', 'head'), may hold values from -6 to 6
- values: bfloat16 [2048, 3072], P('tm', 'head'), may hold values from -6 to 6
- query_gain: float32 [128], replicated, may hold values from 0.25 to 1.75
- key_gain: float32 [128], replicated, may hold values from 0.25 to 1.75
- frames: int32 [4], replicated, may hold values from 1 to 8, 16 in all
- frame_rate: int32 [4], replicated, may hold values from 8 to 30
- out_weight: bfloat16 [24, 3072, 128], P('head', 'tm'), may hold values from -0.109375 to 0.109375
Outputs:
- mixed: bfloat16 [2048, 3072], P('tm', 'head')
The draws below stay inside these ranges and needn't reach their ends.
Inputs may be any that keep to these rules, and one draw needn't show every extreme that they name: The clips' frames, in order, make up all 16 frames; the longest clip has exactly 8 frames.
All inputs are finite; a program needn't handle non-finite values.
Results may differ from the reference program's by a relative error of at most 0.0084.
Values may be sent and summed in bfloat16 or wider, within the bound.
A program may use at most 64 MiB of HBM per device.

```python
import math
import jax
import jax.numpy as jnp
import numpy as np
from jax import lax

D = 3072
H = 24
HD = 128
GW = 16
WIN = 12
NCLIPS = 4
SPAN = 7
FRAME = 128
TOK_DEV = 256
FRAMES = 16
TOKENS = 2048
MAXF = 8


def set_ends(result, key, smallest, largest):
    index_at = [jax.random.randint(jax.random.fold_in(key, axis), (), 0, length) for axis, length in enumerate(result.shape)]
    main_axis = result.shape.index(max(result.shape))
    neighbour = index_at[:main_axis] + [(index_at[main_axis] + 1) % result.shape[main_axis]] + index_at[main_axis + 1:]
    return result.at[tuple(index_at)].set(smallest).at[tuple(neighbour)].set(largest)


def steps_of(key, shape, split, low, largest):
    loudness, own = 1.0, jax.random.fold_in(key, 6)
    for position, shards_of in split:
        steps = jnp.exp(jax.random.uniform(jax.random.fold_in(own, position), (shards_of,), jnp.float32, low / len(split), largest / len(split)))
        loudness = loudness * jnp.repeat(steps, shape[position] // shards_of).reshape([-1 if axis == position else 1 for axis in range(len(shape))])
    return loudness


def profile(number_of, total, most, lean):
    weights = [(1 << 20) // math.isqrt(standing ** lean) + 1 for standing in range(2, number_of + 1)]
    rest, given = total - most - (number_of - 1), [1] * (number_of - 1)
    while rest > 0:
        movable = [i for i in range(number_of - 1) if given[i] < most]
        mass, budget = sum([weights[i] for i in movable]), rest
        for i in movable:
            more = min(most - given[i], max(1, budget * weights[i] // mass), rest)
            given[i] = given[i] + more
            rest = rest - more
    return np.array([most] + given)


def ragged_sizes(rng, number_of, total, most, lean):
    if number_of == 2:
        one = jax.random.randint(rng, (), max(1, total - most), min(most, total - 1) + 1)
        return jnp.stack([one, total - one])
    tallies = jnp.asarray(profile(number_of, total, most, lean), jnp.int32)
    twos = (number_of - 1) // 2
    source_of, sink = tallies[1:1 + 2 * twos:2], tallies[2:2 + 2 * twos:2]
    margin = jnp.minimum(source_of - 1, most - sink)
    moved = jax.random.randint(jax.random.fold_in(rng, 1), (twos,), 0, 1 << 20) % (margin + 1)
    tallies = tallies.at[1:1 + 2 * twos:2].set(source_of - moved).at[2:2 + 2 * twos:2].set(sink + moved)
    return tallies[jax.random.permutation(jax.random.fold_in(rng, 2), number_of)]


def normal_values(own_key, shape, scale, bound, shards=(), held_as=jnp.bfloat16):
    loudness = steps_of(own_key, shape, shards, -0.22, 0.18) if shards else 1.0
    drawn = jax.random.normal(own_key, shape, jnp.float32) * scale * loudness
    return jnp.minimum(jnp.maximum(drawn, -bound), bound).astype(held_as)


def setup_inputs(seed: int = 0) -> dict:
    seeds = jax.random.split(jax.random.key(seed), 9)
    queries = normal_values(seeds[0], (TOKENS, H * HD), 1.0, 6.0, ((0, 8), (1, 4)))
    key_input = normal_values(seeds[1], (TOKENS, H * HD), 1.0, 6.0, ((0, 8), (1, 4)))
    values = normal_values(seeds[2], (TOKENS, H * HD), 1.0, 6.0, ((0, 8), (1, 4)))
    query_gain = jnp.clip(1.0 + 0.15 * jax.random.normal(seeds[3], (HD,), jnp.float32), 0.25, 1.75)
    key_gain = jnp.clip(1.0 + 0.15 * jax.random.normal(seeds[4], (HD,), jnp.float32), 0.25, 1.75)
    frames = ragged_sizes(seeds[5], NCLIPS, FRAMES, MAXF, 2).astype(jnp.int32)
    frame_rate = set_ends(jax.random.randint(seeds[6], (NCLIPS,), 8, 31), jax.random.fold_in(seeds[6], 1), 8, 30).astype(jnp.int32)
    out_weight = normal_values(seeds[7], (H, D, HD), (H * HD) ** -0.5, 0.109375, ((0, 4), (1, 8)))
    return dict(queries=queries, key_input=key_input, values=values, query_gain=query_gain, key_gain=key_gain, frames=frames, frame_rate=frame_rate, out_weight=out_weight)


def rope_freqs(width):
    steps = jnp.arange(width // 2, dtype=jnp.float32)
    return jnp.exp(steps * (-2.0 * math.log(10000.0) / width))

def clip_of(token_index, frames):
    ends = jnp.cumsum(frames).astype(jnp.int32)
    starts = (ends - frames).astype(jnp.int32)
    frame_global = (token_index // FRAME).astype(jnp.int32)
    inside = ((frame_global[:, None] >= starts[None, :]) & (frame_global[:, None] < ends[None, :])).astype(jnp.int32)
    clip_id = lax.optimization_barrier(jnp.sum(inside * jnp.arange(frames.shape[0], dtype=jnp.int32)[None, :], axis=1)).astype(jnp.int32)
    return (clip_id, frame_global, inside, starts)

def rotary(token_index, frames, frame_rate, head_size):
    clip_id, frame_global, inside, starts = clip_of(token_index, frames)
    frame_start = lax.optimization_barrier(jnp.sum(inside * starts[None, :], axis=1)).astype(jnp.int32)
    rate_token = lax.optimization_barrier(jnp.sum(inside * frame_rate[None, :], axis=1)).astype(jnp.float32)
    in_frame = token_index % FRAME
    time_pos = (frame_global - frame_start).astype(jnp.float32) * 24.0 / rate_token
    row_pos = (in_frame // GW).astype(jnp.float32)
    col_pos = (in_frame % GW).astype(jnp.float32)
    side = head_size // 6 * 2
    depth = head_size - 2 * side
    angles = jnp.concatenate([time_pos[:, None] * rope_freqs(depth)[None, :], row_pos[:, None] * rope_freqs(side)[None, :], col_pos[:, None] * rope_freqs(side)[None, :]], axis=1)
    return (clip_id, frame_global, jnp.cos(angles), jnp.sin(angles))

def norm_rotate(rows, gain, cosine, sine):
    values_f = rows.astype(jnp.float32)
    mean_sq = lax.optimization_barrier(jnp.mean(values_f * values_f, axis=-1, keepdims=True))
    normed = values_f * lax.rsqrt(mean_sq + 1e-06) * gain
    half = rows.shape[-1] // 2
    first, second = (normed[..., :half], normed[..., half:])
    cos_b = cosine[:, None, :]
    sin_b = sine[:, None, :]
    return jnp.concatenate([first * cos_b - second * sin_b, second * cos_b + first * sin_b], axis=-1).astype(jnp.bfloat16)

def reference(queries, key_input, values, query_gain, key_gain, frames, frame_rate, out_weight):
    total = queries.shape[0]
    head_count = H
    head_size = HD
    block_rows = TOK_DEV
    index_all = jnp.arange(total, dtype=jnp.int32)
    clip_all, frame_all, cos_all, sin_all = rotary(index_all, frames, frame_rate, head_size)
    q_rot = norm_rotate(queries.reshape(total, head_count, head_size), query_gain, cos_all, sin_all)
    k_rot = norm_rotate(key_input.reshape(total, head_count, head_size), key_gain, cos_all, sin_all)
    v_rows = values.reshape(total, head_count, head_size)
    back = (SPAN - 1) * block_rows
    k_pad = jnp.concatenate([jnp.zeros((back, head_count, head_size), jnp.bfloat16), k_rot], axis=0)
    v_pad = jnp.concatenate([jnp.zeros((back, head_count, head_size), jnp.bfloat16), v_rows], axis=0)
    clip_pad = jnp.concatenate([jnp.full((back,), -1, jnp.int32), clip_all], axis=0)
    frame_pad = jnp.concatenate([jnp.zeros((back,), jnp.int32), frame_all], axis=0)
    w_mat = jnp.transpose(out_weight, (0, 2, 1)).reshape(head_count * head_size, out_weight.shape[1])

    def one_block(block_id):
        first_row = (block_id * block_rows).astype(jnp.int32)
        q_block = lax.dynamic_slice_in_dim(q_rot, first_row, block_rows, 0)
        q_clip = lax.dynamic_slice_in_dim(clip_all, first_row, block_rows, 0)
        q_frame = lax.dynamic_slice_in_dim(frame_all, first_row, block_rows, 0)
        k_block = lax.dynamic_slice_in_dim(k_pad, first_row, SPAN * block_rows, 0)
        v_block = lax.dynamic_slice_in_dim(v_pad, first_row, SPAN * block_rows, 0)
        k_clip = lax.dynamic_slice_in_dim(clip_pad, first_row, SPAN * block_rows, 0)
        k_frame = lax.dynamic_slice_in_dim(frame_pad, first_row, SPAN * block_rows, 0)
        key_mask = (k_clip[None, :] == q_clip[:, None]) & (k_frame[None, :] <= q_frame[:, None]) & (k_frame[None, :] >= q_frame[:, None] - (WIN - 1))
        scores = jnp.einsum('qhe,khe->hqk', q_block.astype(jnp.float32), k_block.astype(jnp.float32)) / math.sqrt(head_size)
        probs = jnp.where(key_mask[None, :, :], jnp.exp(scores), 0.0)
        denom = lax.optimization_barrier(jnp.sum(probs, axis=2))
        probs_b = lax.optimization_barrier(probs.astype(jnp.bfloat16)).astype(jnp.float32)
        numerator = jnp.einsum('hqk,khe->qhe', probs_b, v_block.astype(jnp.float32))
        attended = (numerator / jnp.transpose(denom)[:, :, None]).astype(jnp.bfloat16)
        flat = attended.reshape(block_rows, head_count * head_size)
        return jnp.dot(flat, w_mat, preferred_element_type=jnp.float32).astype(jnp.bfloat16)
    blocks = lax.map(one_block, jnp.arange(total // block_rows, dtype=jnp.int32))
    return blocks.reshape(total, out_weight.shape[1])
```

```python
import functools
import math

import jax
import jax.numpy as jnp
from jax import lax
from jax.experimental import pallas as pl
from jax.experimental.pallas import tpu as pltpu
from jax.sharding import PartitionSpec as P

GW = 16
WIN = 12
FRAME = 128
MESH = pl.DeviceIdType.MESH


def rope_freqs(width):
    steps = jnp.arange(width // 2, dtype=jnp.float32)
    return jnp.exp(steps * (-2.0 * math.log(10000.0) / width))


def clip_of(frame_global, frames):
    count = frames.shape[0]
    upto = jnp.arange(count)[:, None] >= jnp.arange(count)[None, :]
    ends = jnp.sum(jnp.where(upto, frames[None, :], 0), axis=1)
    starts = ends - frames
    inside = (
        (frame_global[:, None] >= starts[None, :]) & (frame_global[:, None] < ends[None, :])
    ).astype(jnp.int32)
    clip_id = jnp.sum(inside * jnp.arange(frames.shape[0], dtype=jnp.int32)[None, :], axis=1)
    return (clip_id, inside, starts)


def rotary(token_index, frames, frame_rate, head_size):
    frame_global = token_index // FRAME
    clip_id, inside, starts = clip_of(frame_global, frames)
    frame_start = jnp.sum(inside * starts[None, :], axis=1)
    rate_token = jnp.sum(inside * frame_rate[None, :], axis=1).astype(jnp.float32)
    in_frame = token_index % FRAME
    time_pos = (frame_global - frame_start).astype(jnp.float32) * 24.0 / rate_token
    row_pos = (in_frame // GW).astype(jnp.float32)
    col_pos = (in_frame % GW).astype(jnp.float32)
    side = head_size // 6 * 2
    depth = head_size - 2 * side
    angles = jnp.concatenate(
        [
            time_pos[:, None] * rope_freqs(depth)[None, :],
            row_pos[:, None] * rope_freqs(side)[None, :],
            col_pos[:, None] * rope_freqs(side)[None, :],
        ],
        axis=1,
    )
    cosine, sine = jnp.cos(angles), jnp.sin(angles)
    return (jnp.concatenate([cosine, cosine], axis=1), jnp.concatenate([-sine, sine], axis=1))


def wide_kernel(cfg, q_hbm, k_hbm, v_hbm, w_hbm, cos_ref, sin_ref, gain_ref, mask_ref, out_ref,
           q_ref, k_ref, v_ref, qd, kb, vb, wg, num, den, ntx, nrx, dtx, drx, att, ptx, keep, rx1, stx, rx2, ytx, yrx,
           qd_s, qd_r, pt_s, pt_r, nu_s, nu_r, wu_s, wu_r, wd_s, wd_r, at_s, at_r,
           c_s, c_r, h_s, h_r, y_s, y_r, loc):
    n_out, reach, steps, q_cnt, heads, hs = cfg
    rows = q_ref.shape[0]
    pos = lax.axis_index("tm")
    head = lax.axis_index("head")
    o, b = pos // 2, pos % 2
    hi, lo = head // 2, head % 2
    partner = pos + 1 - 2 * b
    core = head + 1 - 2 * lo
    cross = lax.rem(head + 2, 4)
    has_up = o + 1 < n_out
    has_dn = o >= 1

    loads = [pltpu.make_async_copy(src, dst, loc.at[i]) for i, (src, dst) in enumerate(
        [(w_hbm, wg.at[o]), (q_hbm, q_ref), (k_hbm, k_ref), (v_hbm, v_ref)])]
    for c in loads:
        c.start()

    barrier = pltpu.get_barrier_semaphore()
    pl.semaphore_signal(barrier, inc=1, device_id={"tm": partner}, device_id_type=MESH)
    pl.semaphore_signal(barrier, inc=1, device_id={"head": core}, device_id_type=MESH)
    pl.semaphore_signal(barrier, inc=1, device_id={"head": cross}, device_id_type=MESH)

    @pl.when(has_up)
    def _():
        pl.semaphore_signal(barrier, inc=1, device_id={"tm": pos + 2}, device_id_type=MESH)

    @pl.when(has_dn)
    def _():
        pl.semaphore_signal(barrier, inc=1, device_id={"tm": pos - 2}, device_id_type=MESH)

    amount = 3 + has_up.astype(jnp.int32) + has_dn.astype(jnp.int32)
    pl.semaphore_wait(barrier, amount)

    def rcopy(src, dst, s, r, axis, index):
        return pltpu.make_async_remote_copy(
            src_ref=src, dst_ref=dst, send_sem=s, recv_sem=r,
            device_id={axis: index}, device_id_type=MESH)

    def q_at(s):
        return q_ref if s == 0 else qd.at[s - 1]

    def q_dn(s):
        return [rcopy(q_at(s - 1), q_at(s), qd_s.at[s - 1], qd_r.at[s - 1], "tm", pos - 2)]

    def n_up(s):
        return [rcopy(ntx.at[s - 1], nrx.at[s - 1], nu_s.at[s - 1, 0], nu_r.at[s - 1, 0],
                      "tm", pos + 2),
                rcopy(dtx.at[s - 1], drx.at[s - 1], nu_s.at[s - 1, 1], nu_r.at[s - 1, 1],
                      "tm", pos + 2)]

    pair_kv = [rcopy(k_ref, kb, pt_s.at[0], pt_r.at[0], "tm", partner),
               rcopy(v_ref, vb, pt_s.at[1], pt_r.at[1], "tm", partner)]

    def w_up(t):
        origin = jnp.maximum(o - t + 1, 0)
        return rcopy(wg.at[origin], wg.at[origin], wu_s.at[t - 1], wu_r.at[t - 1], "tm", pos + 2)

    def w_dn(t):
        origin = jnp.minimum(o + t - 1, n_out - 1)
        return rcopy(wg.at[origin], wg.at[origin], wd_s.at[t - 1], wd_r.at[t - 1], "tm", pos - 2)

    def start_all(cond, copies):
        @pl.when(cond)
        def _():
            for c in copies:
                c.start()

    def wait_recv(cond, copies):
        @pl.when(cond)
        def _():
            for c in copies:
                c.wait_recv()

    def wait_send(cond, copies):
        @pl.when(cond)
        def _():
            for c in copies:
                c.wait_send()

    def up_sends(t):
        return has_up & (o - t + 1 >= 0)

    def dn_sends(t):
        return has_dn & (o + t - 1 < n_out)

    def q_sends(s):
        return has_dn & (o + s - 1 < n_out)

    def n_sends(s):
        return has_up & (o + s < n_out)

    def n_gets(s):
        return has_dn & (o + s < n_out)

    scale = 1.0 / math.sqrt(hs)
    lane = lax.broadcasted_iota(jnp.int32, (rows, 128), 1)

    def attend(s, key_ref, value_ref, slot, first):
        query_ref = q_at(s)
        mask = jnp.concatenate(
            [jnp.broadcast_to(mask_ref[slot, f:f + 1, :], (FRAME, rows))
             for f in range(rows // FRAME)], axis=0)
        if first:
            den[s] = jnp.zeros((rows, 128), jnp.float32)

        def one(h, carry):
            at = pl.ds(pl.multiple_of(h * hs, hs), hs)
            scores = lax.dot_general(query_ref[:, at], key_ref[:, at], (((1,), (1,)), ((), ())),
                                     preferred_element_type=jnp.float32)
            probs = jnp.exp(scores * scale) * mask
            total = jnp.sum(probs, axis=1, keepdims=True)
            part = jnp.dot(probs.astype(jnp.bfloat16), value_ref[:, at],
                           preferred_element_type=jnp.float32)
            den[s] += jnp.where(lane == h, total, 0.0)
            if first:
                num[s, :, at] = part
            else:
                num[s, :, at] += part
            return carry

        lax.fori_loop(0, heads, one, 0)

    def rotate(ref, row):
        gain = gain_ref[row:row + 1, :]
        for h in range(heads):
            at = slice(h * hs, (h + 1) * hs)
            x = ref[:, at].astype(jnp.float32)
            mean_sq = jnp.mean(x * x, axis=1, keepdims=True)
            x = x * lax.rsqrt(mean_sq + 1e-06) * gain
            ref[:, at] = (x * cos_ref[...]
                          + pltpu.roll(x, hs // 2, 1) * sin_ref[...]).astype(jnp.bfloat16)

    loads[0].wait()
    start_all(up_sends(1), [w_up(1)])
    loads[3].wait()
    pair_kv[1].start()
    loads[1].wait()
    rotate(q_ref, 0)
    start_all(q_sends(1), q_dn(1))
    loads[2].wait()
    rotate(k_ref, 1)
    pair_kv[0].start()
    attend(0, k_ref, v_ref, 0, True)

    def down(t):
        wait_recv(o + t < n_out, [w_dn(t)])
        if t + 1 < n_out:
            start_all(dn_sends(t + 1), [w_dn(t + 1)])

    def up(t):
        wait_recv(o - t >= 0, [w_up(t)])
        if t + 1 < n_out:
            start_all(up_sends(t + 1), [w_up(t + 1)])

    for s in range(1, steps + 1):
        wait_recv(o + s < n_out, q_dn(s))
        if s < steps:
            start_all(q_sends(s + 1), q_dn(s + 1))
        if s == max(steps - 1, 1):
            start_all(dn_sends(1), [w_dn(1)])

        @pl.when(o + s < n_out)
        def _():
            attend(s, k_ref, v_ref, 2 * s, True)
        if s == 1:
            up(1)
    for c in pair_kv:
        c.wait_recv()

    def with_pair(s):
        cond = (o + s < n_out) & (((b == 0) & (s >= 1)) | ((b == 1) & (2 * s + 1 <= reach)))

        @pl.when(cond)
        def _():
            attend(s, kb, vb, 2 * s + 1, False)

    def add_up(s):
        if s < steps:
            @pl.when(n_gets(s))
            def _():
                for c in n_up(s + 1):
                    c.wait_recv()
                num[s] += nrx[s].astype(jnp.float32)
                wide = jnp.concatenate(
                    [drx[s], jnp.zeros((120, rows), jnp.float32)], axis=0)
                den[s] += jnp.transpose(wide)
        if s >= 1:
            @pl.when(n_sends(s))
            def _():
                ntx[s - 1] = num[s].astype(jnp.bfloat16)
                dtx[s - 1] = jnp.transpose(den[s])[0:8]
                for c in n_up(s):
                    c.start()

    with_pair(steps)
    add_up(steps)
    for s in range(steps - 1, -1, -1):
        with_pair(s)
    up(2)
    down(1)
    for s in range(steps - 1, -1, -1):
        if s == 0:
            down(2)
        add_up(s)

    for h in range(heads):
        at = slice(h * hs, (h + 1) * hs)
        att[0:rows, at] = (num[0, :, at] / den[0, :, h:h + 1]).astype(jnp.bfloat16)
    swap = rcopy(att.at[pl.ds(0, rows)], att.at[pl.ds(rows, rows)], at_s, at_r, "tm", partner)
    swap.start()
    for t in range(3, n_out):
        down(t)
        up(t)
    swap.wait_recv()

    def project(group, store):
        def one(k, carry):
            weight = jnp.concatenate([wg[group * q_cnt + k, h] for h in range(heads)], axis=1)
            acc = lax.dot_general(att[...], weight, (((1,), (1,)), ((), ())),
                                  preferred_element_type=jnp.float32)
            store(k, acc)
            return carry
        if q_cnt == 1:
            one(0, 0)
        else:
            lax.fori_loop(0, q_cnt, one, 0)

    sides = (1 - hi, hi)
    c_copies = []
    for i, side in enumerate(sides):
        def put(k, acc, i=i):
            ptx[i, k] = acc.astype(jnp.bfloat16)
        project(2 * side + (1 - lo), put)
        copy = rcopy(ptx.at[i], rx1.at[i], c_s.at[i], c_r.at[i], "head", core)
        copy.start()
        c_copies.append(copy)
    for i, side in enumerate(sides):
        def put(k, acc, i=i):
            keep[i, k] = acc
        project(2 * side + lo, put)
    c_copies[0].wait_recv()
    h_copies = [None, None]
    for r in (1, 0):
        at = slice(r * rows, (r + 1) * rows)
        stx[r] = (keep[0, :, at] + rx1[0, :, at].astype(jnp.float32)).astype(jnp.bfloat16)
        h_copies[r] = rcopy(stx.at[r], rx2.at[r], h_s.at[r], h_r.at[r], "head", cross)
        h_copies[r].start()
    c_copies[1].wait_recv()

    def final(r):
        at = slice(r * rows, (r + 1) * rows)
        mine = keep[1, :, at] + rx1[1, :, at].astype(jnp.float32)
        return (mine + rx2[r].astype(jnp.float32)).astype(jnp.bfloat16)

    h_copies[1].wait_recv()
    ytx[...] = final(1)
    y_copy = rcopy(ytx, yrx, y_s, y_r, "tm", partner)
    y_copy.start()
    h_copies[0].wait_recv()
    if len(out_ref.shape) == 2:
        dsl = ytx.shape[-1]
        out_ref[:, pl.ds(pl.multiple_of(b * dsl, 128), dsl)] = final(0)[0]
        y_copy.wait_recv()
        out_ref[:, pl.ds(pl.multiple_of((1 - b) * dsl, 128), dsl)] = yrx[0]
    else:
        out_ref[b] = final(0)
        y_copy.wait_recv()
        out_ref[1 - b] = yrx[...]

    for c in pair_kv:
        c.wait_send()
    for s in range(1, steps + 1):
        wait_send(q_sends(s), q_dn(s))
        wait_send(n_sends(s), n_up(s))
    for t in range(1, n_out):
        wait_send(up_sends(t), [w_up(t)])
        wait_send(dn_sends(t), [w_dn(t)])
    for c in [swap, y_copy] + c_copies + h_copies:
        c.wait_send()


def wide_device(queries, key_input, values, query_gain, key_gain, frames, frame_rate, out_weight):
    rows = queries.shape[0]
    hs = query_gain.shape[0]
    heads = queries.shape[1] // hs
    n = lax.axis_size("tm")
    m = lax.axis_size("head")
    n_out = n // 2
    per = rows // FRAME
    longest = n * per // 2
    back = min(WIN, longest) - 1
    reach = min((back + per - 1) // per, n - 1)
    steps = (reach + 1) // 2
    q_cnt = n_out // m
    dsl = out_weight.shape[1]

    pos = lax.axis_index("tm")
    b = pos % 2
    own_index = pos * rows + jnp.arange(rows, dtype=jnp.int32)
    cosine, sine = rotary(own_index, frames, frame_rate, hs)
    gains = jnp.stack([query_gain, key_gain])

    frames_at = jnp.arange(per, dtype=jnp.int32)
    q_pos = jnp.stack([pos + 2 * (slot // 2) for slot in range(2 * steps + 2)])
    k_pos = jnp.stack([pos, pos + 1 - 2 * b] * (steps + 1))
    q_frame = q_pos[:, None] * per + frames_at[None, :]
    q_clip = clip_of(q_frame.reshape(-1), frames)[0].reshape(q_frame.shape)
    k_frame = (k_pos[:, None] * per
               + (jnp.arange(rows, dtype=jnp.int32) // FRAME)[None, :])
    k_clip = clip_of(k_frame.reshape(-1), frames)[0].reshape(k_frame.shape)
    kf, kc = k_frame[:, None, :], k_clip[:, None, :]
    qf, qc = q_frame[:, :, None], q_clip[:, :, None]
    mask = ((kc == qc) & (kf <= qf) & (kf >= qf - (WIN - 1))).astype(jnp.float32)

    bf, f32 = jnp.bfloat16, jnp.float32
    width = heads * hs
    flat = q_cnt == 1 and dsl % 128 == 0
    shape = (rows, 2 * dsl) if flat else (2, q_cnt, rows, dsl)
    dma = pltpu.SemaphoreType.DMA
    out = pl.pallas_call(
        functools.partial(wide_kernel, (n_out, reach, steps, q_cnt, heads, hs)),
        out_shape=jax.ShapeDtypeStruct(shape, bf),
        in_specs=[pl.BlockSpec(memory_space=pl.ANY)] * 4
        + [pl.BlockSpec(memory_space=pltpu.VMEM)] * 4,
        out_specs=pl.BlockSpec(memory_space=pltpu.VMEM),
        scratch_shapes=[
            pltpu.VMEM((rows, width), bf),
            pltpu.VMEM((rows, width), bf),
            pltpu.VMEM((rows, width), bf),
            pltpu.VMEM((steps, rows, width), bf),
            pltpu.VMEM((rows, width), bf),
            pltpu.VMEM((rows, width), bf),
            pltpu.VMEM((n_out,) + out_weight.shape, bf),
            pltpu.VMEM((steps + 1, rows, width), f32),
            pltpu.VMEM((steps + 1, rows, 128), f32),
            pltpu.VMEM((steps, rows, width), bf),
            pltpu.VMEM((steps, rows, width), bf),
            pltpu.VMEM((steps, 8, rows), f32),
            pltpu.VMEM((steps, 8, rows), f32),
            pltpu.VMEM((2 * rows, width), bf),
            pltpu.VMEM((2, q_cnt, 2 * rows, dsl), bf),
            pltpu.VMEM((2, q_cnt, 2 * rows, dsl), f32),
            pltpu.VMEM((2, q_cnt, 2 * rows, dsl), bf),
            pltpu.VMEM((2, q_cnt, rows, dsl), bf),
            pltpu.VMEM((2, q_cnt, rows, dsl), bf),
            pltpu.VMEM((q_cnt, rows, dsl), bf),
            pltpu.VMEM((q_cnt, rows, dsl), bf),
            dma((steps,)), dma((steps,)), dma((2,)), dma((2,)), dma((steps, 2)), dma((steps, 2)),
            dma((n_out - 1,)), dma((n_out - 1,)), dma((n_out - 1,)), dma((n_out - 1,)),
            dma, dma, dma((2,)), dma((2,)), dma((2,)), dma((2,)), dma, dma, dma((4,)),
        ],
        compiler_params=pltpu.CompilerParams(
            collective_id=0, has_side_effects=True, vmem_limit_bytes=56 * 1024 * 1024
        ),
    )(queries, key_input, values, out_weight, cosine, sine, gains, mask)
    if flat:
        return out
    return jnp.transpose(out, (2, 1, 0, 3)).reshape(rows, 2 * q_cnt * dsl)


def level_kernel(cfg, frames_ref, rate_ref, q_hbm, k_hbm, v_hbm, w_hbm, qg_ref, kg_ref, out_ref,
                 q_in, k_in, cosine, sine, mask_ref, qtx, ktx, qx, kx, vx, num, den,
                 ntx, dtx, nrx, drx, att, wg, ptx, prx, keep, stx, xrx, ytx, yrx,
                 loc, ex_s, ex_r, qd_s, qd_r, kv_s, kv_r, nu_s, nu_r, at_s, at_r,
                 wu_s, wu_r, wd_s, wd_r, c_s, c_r, x_s, x_r, y_s, y_r):
    hs, mine, clips = cfg
    rows = q_in.shape[0]
    level = 2 * rows
    per = level // FRAME
    bf, f32, i32 = jnp.bfloat16, jnp.float32, jnp.int32
    pos = lax.axis_index("tm")
    head = lax.axis_index("head")
    z, y = pos // 2, pos % 2
    x, c = head // 2, head % 2
    partner = {"tm": pos + 1 - 2 * y}
    sibling = {"head": head + 1 - 2 * c}
    cross = {"head": lax.rem(head + 2, 4)}
    above = {"tm": pos + 2}
    below = {"tm": pos - 2}

    def lanes(i, n):
        return pl.ds(pl.multiple_of(i * n, hs), n)

    def half(i, base=0):
        return pl.ds(pl.multiple_of(base + i * rows, rows), rows)

    own_rows, other_rows = half(y), half(1 - y)

    def local(src, dst, i):
        return pltpu.make_async_copy(src, dst, loc.at[i])

    load_q = local(q_hbm, q_in, 0)
    load_k = local(k_hbm, k_in, 1)
    load_w = local(w_hbm, wg.at[z], 2)
    load_v = [local(v_hbm.at[:, lanes(mine * y + h, hs)], vx.at[h, half(y, level)], 3 + h)
              for h in range(mine)]
    for load in [load_q, load_k, load_w] + load_v:
        load.start()

    barrier = pltpu.get_barrier_semaphore()
    for near in (partner, sibling, cross):
        pl.semaphore_signal(barrier, inc=1, device_id=near, device_id_type=MESH)

    @pl.when(z < 3)
    def _():
        pl.semaphore_signal(barrier, inc=1, device_id=above, device_id_type=MESH)

    @pl.when(z > 0)
    def _():
        pl.semaphore_signal(barrier, inc=1, device_id=below, device_id_type=MESH)

    def rcopy(src, dst, s, r, where):
        return pltpu.make_async_remote_copy(
            src_ref=src, dst_ref=dst, send_sem=s, recv_sem=r,
            device_id=where, device_id_type=MESH)

    def q_ex(h):
        return rcopy(qtx.at[h], qx.at[0, h, own_rows], ex_s.at[0, h], ex_r.at[0, h], partner)

    def k_ex(h):
        return rcopy(ktx.at[h], kx.at[h, half(y, level)], ex_s.at[1, h], ex_r.at[1, h], partner)

    def v_ex(h):
        return rcopy(v_hbm.at[:, lanes(mine * (1 - y) + h, hs)], vx.at[h, half(y, level)],
                     ex_s.at[2, h], ex_r.at[2, h], partner)

    def q_dn(i, h):
        at = half(y) if i == 0 else half(1 - y)
        return rcopy(qx.at[0, h, at], qx.at[1, h, at], qd_s.at[i, h], qd_r.at[i, h], below)

    part = level - FRAME

    def q_fw(h):
        at = pl.ds(0, part)
        return rcopy(qx.at[1, h, at], qx.at[2, h, at], qd_s.at[2, h], qd_r.at[2, h], below)

    def kv_up(n, h):
        ref, i = (kx, vx)[n % 2], (y, 1 - y)[n // 2]
        return rcopy(ref.at[h, half(i, level)], ref.at[h, half(i)], kv_s.at[n, h], kv_r.at[n, h],
                     above)

    def n_up(s, h):
        return [rcopy(ntx.at[s, h], nrx.at[s, h], nu_s.at[s, 0, h], nu_r.at[s, 0, h], above),
                rcopy(dtx.at[s, h], drx.at[s, h], nu_s.at[s, 1, h], nu_r.at[s, 1, h], above)]

    def swap(h):
        at = att.at[mine * y + h]
        return rcopy(at, at, at_s.at[h], at_r.at[h], partner)

    def w_own(j):
        return w_hbm.at[:, pl.ds(j * hs, hs), :]

    def w_piece(o, j):
        return wg.at[o, :, pl.ds(pl.multiple_of(j * hs, hs), hs), :]

    def w_up(o, j, own=False):
        return rcopy(w_own(j) if own else w_piece(o, j), w_piece(o, j), wu_s.at[o, j], wu_r.at[o, j], above)

    def w_dn(o, j, own=False):
        return rcopy(w_own(j) if own else w_piece(o, j), w_piece(o, j), wd_s.at[o, j], wd_r.at[o, j], below)

    pieces = 3

    shape = (2 * 8, hs)
    lane = lax.broadcasted_iota(i32, shape, 1)
    sub = lax.broadcasted_iota(i32, shape, 0)
    pair = jnp.where(lane >= hs // 2, lane - hs // 2, lane)
    side = hs // 6 * 2
    depth = hs - 2 * side
    in_t = pair < depth // 2
    in_h = (pair >= depth // 2) & (pair < depth // 2 + side // 2)
    step = jnp.where(in_t, pair, jnp.where(in_h, pair - depth // 2, pair - depth // 2 - side // 2))
    log = -2.0 * math.log(10000.0)
    freq = jnp.exp(step.astype(f32) * jnp.where(in_t, log / depth, log / side))
    times = []
    for i in range(2):
        frame = 2 * pos + i
        end, start, rate = i32(0), i32(0), i32(0)
        for n in range(clips):
            inside = (frame >= end) & (frame < end + frames_ref[n])
            start = jnp.where(inside, end, start)
            rate = jnp.where(inside, rate_ref[n], rate)
            end = end + frames_ref[n]
        times.append(jnp.full(shape, frame - start, i32).astype(f32) * 24.0
                     / jnp.full(shape, rate, i32).astype(f32))
    sub8 = jnp.where(sub >= 8, sub - 8, sub)
    place = jnp.where(in_t, jnp.where(sub < 8, times[0], times[1]),
                      jnp.where(in_h, sub8, sub).astype(f32))
    angle = place * freq
    cos16 = jnp.cos(angle)
    sin16 = jnp.sin(angle) * jnp.where(lane < hs // 2, -1.0, 1.0)
    for table, small in ((cosine, cos16), (sine, sin16)):
        for i in range(2):
            for r in range(8):
                at = (8 * i + r) * GW
                table[at:at + GW, :] = jnp.where(
                    in_t, jnp.broadcast_to(small[8 * i:8 * i + 1], shape),
                    jnp.where(in_h, jnp.broadcast_to(small[r:r + 1], shape), small))

    def clip_index(frame):
        end, index = i32(0), jnp.zeros(frame.shape, i32)
        for n in range(clips):
            end = end + frames_ref[n]
            index = index + jnp.where(frame >= end, 1, 0)
        return index

    mshape = mask_ref.shape
    q_frame = per * z + lax.broadcasted_iota(i32, mshape, 0)
    k_frame = per * (z - 1) + lax.broadcasted_iota(i32, mshape, 1) // FRAME
    seen = ((clip_index(q_frame) == clip_index(k_frame)) & (k_frame <= q_frame)
            & (k_frame >= q_frame - (WIN - 1)))
    mask_ref[...] = jnp.where(seen, 1.0, 0.0)

    def rotate(src, gain_ref, i, h):
        v = src[:, lanes(mine * i + h, hs)].astype(f32)
        v = v * lax.rsqrt(jnp.mean(v * v, axis=1, keepdims=True) + 1e-06) * gain_ref[...]
        return (v * cosine[...] + pltpu.roll(v, hs // 2, 1) * sine[...]).astype(bf)

    def each(body):
        def step(h, carry):
            body(h)
            return carry
        lax.fori_loop(0, mine, step, 0)

    load_q.wait()
    load_k.wait()
    for load in load_v:
        load.wait()
    amount = 3 + (z < 3).astype(i32) + (z > 0).astype(i32)
    pl.semaphore_wait(barrier, amount)

    @pl.when(z < 3)
    def _():
        w_up(z, 0, True).start()

    @pl.when((z == 1) | (z == 2))
    def _():
        for j in range(1, pieces):
            w_up(z, j, True).start()

    @pl.when(z == 1)
    def _():
        for j in range(pieces):
            w_dn(1, j, True).start()

    def spread(h):
        qtx[h] = rotate(q_in, qg_ref, 1 - y, h)
        q_ex(h).start()
        ktx[h] = rotate(k_in, kg_ref, 1 - y, h)
        k_ex(h).start()
        v_ex(h).start()
        qx[0, h, own_rows, :] = rotate(q_in, qg_ref, y, h)

        @pl.when(z >= 2)
        def _():
            q_dn(0, h).start()
        kx[h, half(y, level), :] = rotate(k_in, kg_ref, y, h)

        @pl.when(z == 0)
        def _():
            kv_up(0, h).start()
            kv_up(1, h).start()

    each(spread)
    load_w.wait()

    scale = math.log2(math.e) / math.sqrt(hs)

    def attend(h, slot, block, k0, klen, first, n=rows):
        at = pl.ds(rows * block, n)
        f0 = per * slot + (rows // FRAME) * block
        keys = slice(k0, k0 + klen)
        mask = jnp.concatenate(
            [jnp.broadcast_to(mask_ref[f0 + f:f0 + f + 1, keys], (FRAME, klen))
             for f in range(n // FRAME)], axis=0)
        ones = jnp.ones((klen, hs), bf)
        scores = lax.dot_general(qx[slot, h, at, :], kx[h, keys, :], (((1,), (1,)), ((), ())),
                                 preferred_element_type=f32)
        probs = (jnp.exp2(scores * scale) * mask).astype(bf)
        both = jnp.dot(probs, jnp.concatenate([vx[h, keys, :], ones], axis=1),
                       preferred_element_type=f32)
        if first:
            num[slot, h, at, :] = both[:, :hs]
            den[slot, h, at, :] = both[:, hs:]
        else:
            num[slot, h, at, :] += both[:, :hs]
            den[slot, h, at, :] += both[:, hs:]

    def attend_own(h):
        q_ex(h).wait_recv()
        k_ex(h).wait_recv()
        v_ex(h).wait_recv()
        attend(h, 0, 0, level, rows, True)
        attend(h, 0, 1, level, level, True)

    def attend_next(h):
        attend(h, 1, 0, level, level, True)
        attend(h, 1, 1, level, level, True)

    def send_sums(slot, h):
        s = slot - 1
        ntx[s, h] = num[slot, h].astype(bf)
        dtx[s, h] = jnp.transpose(den[slot, h])[0:8]
        for copy in n_up(s, h):
            copy.start()

    def add_sums(s, slot, h):
        for copy in n_up(s, h):
            copy.wait_recv()
        num[slot, h] += nrx[s, h].astype(f32)
        den[slot, h] += jnp.transpose(jnp.concatenate([drx[s, h]] * (hs // 8), axis=0))

    def finish(h):
        att[mine * y + h] = (num[0, h] / den[0, h]).astype(bf)
        swap(h).start()

    @pl.when(z == 0)
    def _():
        def pass_on(h):
            k_ex(h).wait_recv()
            kv_up(2, h).start()
            v_ex(h).wait_recv()
            kv_up(3, h).start()

        def rest(h):
            q_ex(h).wait_recv()
            attend(h, 0, 0, level, rows, True)
            attend(h, 0, 1, level, level, True)
            finish(h)

        each(pass_on)
        each(rest)
        for j in range(1, pieces):
            w_up(0, j, True).start()

    @pl.when(z == 1)
    def _():
        w_up(0, 0).wait_recv()
        w_up(0, 0).start()
        each(attend_own)

        def one_above(h):
            q_dn(0, h).wait_recv()
            q_dn(1, h).wait_recv()
            attend_next(h)

        def two_above(h):
            q_fw(h).wait_recv()
            attend(h, 2, 0, level, level, True)
            attend(h, 2, 1, level + rows, rows, True, FRAME)
            num[2, h, part:level] = jnp.zeros((FRAME, hs), f32)
            den[2, h, part:level] = jnp.zeros((FRAME, hs), f32)
            send_sums(2, h)

        def from_below(h):
            for n in range(4):
                kv_up(n, h).wait_recv()
            attend(h, 1, 0, 0, level, False)
            attend(h, 1, 1, rows, rows, False)
            send_sums(1, h)

        def own_below(h):
            attend(h, 0, 0, 0, level, False)
            attend(h, 0, 1, 0, level, False)
            finish(h)

        each(one_above)
        each(two_above)
        each(from_below)
        each(own_below)

    @pl.when(z == 2)
    def _():
        def pass_on(h):
            q_ex(h).wait_recv()
            q_dn(1, h).start()
            q_dn(0, h).wait_recv()
            q_dn(1, h).wait_recv()
            q_fw(h).start()

        def own(h):
            k_ex(h).wait_recv()
            v_ex(h).wait_recv()
            attend(h, 0, 0, level, rows, True)
            attend(h, 0, 1, level, level, True)

        def two_below(h):
            add_sums(1, 1, h)
            send_sums(1, h)

        def last(h):
            add_sums(0, 0, h)
            finish(h)

        each(pass_on)
        for j in range(pieces):
            w_up(1, j).wait_recv()
            w_up(1, j).start()
        each(own)
        each(attend_next)
        for j in range(pieces):
            w_dn(2, j, True).start()
        each(two_below)
        for j in range(pieces):
            w_dn(3, j).wait_recv()
            w_dn(3, j).start()
        each(last)

    @pl.when(z == 3)
    def _():
        def pass_on(h):
            q_ex(h).wait_recv()
            q_dn(1, h).start()

        def own(h):
            k_ex(h).wait_recv()
            v_ex(h).wait_recv()
            attend(h, 0, 0, level, rows, True)
            attend(h, 0, 1, level, level, True)

        def last(h):
            add_sums(0, 0, h)
            finish(h)

        each(pass_on)
        for j in range(pieces):
            w_dn(3, j, True).start()
        each(own)
        each(last)

    for h in range(mine):
        swap(h).wait_recv()

    def order(n):
        t, j = n // pieces, n % pieces
        low = jnp.where((z == 1) | (z == 2), jnp.where(t < 2, 1 - t, t), t)
        o = jnp.where(z < 2, low, 3 - low)
        return o, j

    def project(n, carry):
        @pl.when(n < 4 * pieces)
        def _():
            o, j = order(n)
            seen = ((z == 1) & (o == 0) & (j == 0)) | ((z == 2) & ((o == 1) | (o == 3)))

            @pl.when((o < z) & ~seen)
            def _():
                w_up(o, j).wait_recv()

                @pl.when(z < 3)
                def _():
                    w_up(o, j).start()

            @pl.when((o > z) & ~seen)
            def _():
                w_dn(o, j).wait_recv()

                @pl.when(z > 0)
                def _():
                    w_dn(o, j).start()

            weight = jnp.concatenate(
                [wg[o, h, pl.ds(pl.multiple_of(j * hs, hs), hs), :] for h in range(2 * mine)], axis=1)
            rows_in = jnp.concatenate([att[h] for h in range(2 * mine)], axis=1)
            acc = lax.dot_general(rows_in, weight, (((1,), (1,)), ((), ())),
                                  preferred_element_type=f32)
            m = (o // 2) * pieces + j

            @pl.when(o % 2 != c)
            def _():
                ptx[m] = acc.astype(bf)
                rcopy(ptx.at[m], prx.at[m], c_s.at[m], c_r.at[m], sibling).start()

            @pl.when(o % 2 == c)
            def _():
                keep[m] = acc

        o1, j1 = order(n - 1)

        @pl.when((n >= 1) & (n <= 4 * pieces) & (o1 % 2 == c))
        def _():
            m = (o1 // 2) * pieces + j1
            rcopy(ptx.at[m], prx.at[m], c_s.at[m], c_r.at[m], sibling).wait_recv()

            @pl.when(o1 // 2 != x)
            def _():
                stx[j1] = (keep[m] + prx[m].astype(f32)).astype(bf)
                rcopy(stx.at[j1], xrx.at[j1], x_s.at[j1], x_r.at[j1], cross).start()

            @pl.when(o1 // 2 == x)
            def _():
                keep[m] = keep[m] + prx[m].astype(f32)

        return carry

    lax.fori_loop(0, 4 * pieces + 1, project, 0)

    def last(j, carry):
        m = (head // 2) * pieces + j
        rcopy(stx.at[j], xrx.at[j], x_s.at[j], x_r.at[j], cross).wait_recv()
        ytx[j] = (keep[m, other_rows, :] + xrx[j, other_rows, :].astype(f32)).astype(bf)
        rcopy(ytx.at[j], yrx.at[j], y_s.at[j], y_r.at[j], partner).start()
        out_ref[:, lanes(pieces * y + j, hs)] = (
            keep[m, own_rows, :] + xrx[j, own_rows, :].astype(f32)).astype(bf)
        return carry

    lax.fori_loop(0, pieces, last, 0)

    for j in range(pieces):
        copy = rcopy(ytx.at[j], yrx.at[j], y_s.at[j], y_r.at[j], partner)
        copy.wait_recv()
        out_ref[:, lanes(pieces * (1 - y) + j, hs)] = yrx[j]

    def sent(h):
        for copy in (q_ex(h), k_ex(h), v_ex(h), swap(h)):
            copy.wait_send()

        @pl.when(z >= 2)
        def _():
            q_dn(0, h).wait_send()
            q_dn(1, h).wait_send()

        @pl.when(z == 2)
        def _():
            q_fw(h).wait_send()

        @pl.when(z == 0)
        def _():
            for n in range(4):
                kv_up(n, h).wait_send()

        @pl.when((z == 1) | (z == 2))
        def _():
            for copy in n_up(0, h):
                copy.wait_send()

        @pl.when(z == 1)
        def _():
            for copy in n_up(1, h):
                copy.wait_send()

    each(sent)

    for o in range(4):
        @pl.when((z < 3) & (z >= o))
        def _():
            for j in range(pieces):
                w_up(o, j).wait_send()

        @pl.when((z > 0) & (z <= o))
        def _():
            for j in range(pieces):
                w_dn(o, j).wait_send()
    for m in range(2 * pieces):
        rcopy(ptx.at[m], prx.at[m], c_s.at[m], c_r.at[m], sibling).wait_send()
    for j in range(pieces):
        rcopy(stx.at[j], xrx.at[j], x_s.at[j], x_r.at[j], cross).wait_send()
        rcopy(ytx.at[j], yrx.at[j], y_s.at[j], y_r.at[j], partner).wait_send()


def level_device(queries, key_input, values, query_gain, key_gain, frames, frame_rate, out_weight):
    rows, width = queries.shape
    hs = query_gain.shape[0]
    mine = width // hs // 2
    level = 2 * rows
    pieces = out_weight.shape[1] // hs
    bf, f32 = jnp.bfloat16, jnp.float32
    dma = pltpu.SemaphoreType.DMA
    vmem = pltpu.VMEM
    smem = pl.BlockSpec(memory_space=pltpu.SMEM)
    near = pl.BlockSpec(memory_space=pltpu.VMEM)
    far = pl.BlockSpec(memory_space=pl.ANY)
    return pl.pallas_call(
        functools.partial(level_kernel, (hs, mine, frames.shape[0])),
        out_shape=jax.ShapeDtypeStruct((rows, width), bf),
        in_specs=[smem, smem, far, far, far, far, near, near],
        out_specs=near,
        scratch_shapes=[
            vmem((rows, width), bf), vmem((rows, width), bf),
            vmem((rows, hs), f32), vmem((rows, hs), f32),
            vmem((16, 2 * level), f32),
            vmem((mine, rows, hs), bf), vmem((mine, rows, hs), bf),
            vmem((3, mine, level, hs), bf),
            vmem((mine, 2 * level, hs), bf), vmem((mine, 2 * level, hs), bf),
            vmem((3, mine, level, hs), f32), vmem((3, mine, level, hs), f32),
            vmem((2, mine, level, hs), bf), vmem((2, mine, 8, level), f32),
            vmem((2, mine, level, hs), bf), vmem((2, mine, 8, level), f32),
            vmem((2 * mine, level, hs), bf),
            vmem((4,) + out_weight.shape, bf),
            vmem((2 * pieces, level, hs), bf), vmem((2 * pieces, level, hs), bf),
            vmem((2 * pieces, level, hs), f32),
            vmem((pieces, level, hs), bf), vmem((pieces, level, hs), bf),
            vmem((pieces, rows, hs), bf), vmem((pieces, rows, hs), bf),
            dma((3 + mine,)), dma((3, mine)), dma((3, mine)), dma((3, mine)), dma((3, mine)),
            dma((4, mine)), dma((4, mine)), dma((2, 2, mine)), dma((2, 2, mine)),
            dma((mine,)), dma((mine,)),
            dma((4, pieces)), dma((4, pieces)), dma((4, pieces)), dma((4, pieces)),
            dma((2 * pieces,)), dma((2 * pieces,)), dma((pieces,)), dma((pieces,)),
            dma((pieces,)), dma((pieces,)),
        ],
        compiler_params=pltpu.CompilerParams(
            collective_id=0, has_side_effects=True, vmem_limit_bytes=56 * 1024 * 1024
        ),
    )(frames, frame_rate, queries, key_input, values, out_weight,
      query_gain.reshape(1, hs), key_gain.reshape(1, hs))


def per_device(queries, key_input, values, query_gain, key_gain, frames, frame_rate, out_weight):
    args = (queries, key_input, values, query_gain, key_gain, frames, frame_rate, out_weight)
    rows, width = queries.shape
    heads, columns, hs = out_weight.shape
    fits = (lax.axis_size("tm") == 8 and lax.axis_size("head") == 4 and rows == 2 * FRAME
            and FRAME == 8 * GW and hs == 128 and heads % 2 == 0
            and columns == width // 2 == 3 * hs)
    if fits:
        return level_device(*args)
    return wide_device(*args)


def solution(mesh):
    in_specs = (
        P("tm", "head"),
        P("tm", "head"),
        P("tm", "head"),
        P(),
        P(),
        P(),
        P(),
        P("head", "tm", None),
    )
    out_specs = P("tm", "head")
    return jax.shard_map(
        per_device, mesh=mesh, in_specs=in_specs, out_specs=out_specs, check_vma=False
    )
```

```python
import functools
import math

import jax
import jax.numpy as jnp
from jax import lax
from jax.experimental import pallas as pl
from jax.experimental.pallas import tpu as pltpu
from jax.sharding import PartitionSpec as P

GW = 16
WIN = 12
FRAME = 128
MESH = pl.DeviceIdType.MESH


def rope_freqs(width):
    steps = jnp.arange(width // 2, dtype=jnp.float32)
    return jnp.exp(steps * (-2.0 * math.log(10000.0) / width))


def clip_of(frame_global, frames):
    count = frames.shape[0]
    upto = jnp.arange(count)[:, None] >= jnp.arange(count)[None, :]
    ends = jnp.sum(jnp.where(upto, frames[None, :], 0), axis=1)
    starts = ends - frames
    inside = (
        (frame_global[:, None] >= starts[None, :]) & (frame_global[:, None] < ends[None, :])
    ).astype(jnp.int32)
    clip_id = jnp.sum(inside * jnp.arange(frames.shape[0], dtype=jnp.int32)[None, :], axis=1)
    return (clip_id, inside, starts)


def rotary(token_index, frames, frame_rate, head_size):
    frame_global = token_index // FRAME
    clip_id, inside, starts = clip_of(frame_global, frames)
    frame_start = jnp.sum(inside * starts[None, :], axis=1)
    rate_token = jnp.sum(inside * frame_rate[None, :], axis=1).astype(jnp.float32)
    in_frame = token_index % FRAME
    time_pos = (frame_global - frame_start).astype(jnp.float32) * 24.0 / rate_token
    row_pos = (in_frame // GW).astype(jnp.float32)
    col_pos = (in_frame % GW).astype(jnp.float32)
    side = head_size // 6 * 2
    depth = head_size - 2 * side
    angles = jnp.concatenate(
        [
            time_pos[:, None] * rope_freqs(depth)[None, :],
            row_pos[:, None] * rope_freqs(side)[None, :],
            col_pos[:, None] * rope_freqs(side)[None, :],
        ],
        axis=1,
    )
    cosine, sine = jnp.cos(angles), jnp.sin(angles)
    return (jnp.concatenate([cosine, cosine], axis=1), jnp.concatenate([-sine, sine], axis=1))


def wide_kernel(cfg, q_hbm, k_hbm, v_hbm, w_hbm, cos_ref, sin_ref, gain_ref, mask_ref, out_ref,
           q_ref, k_ref, v_ref, qd, kb, vb, wg, num, den, ntx, nrx, dtx, drx, att, ptx, keep, rx1, stx, rx2, ytx, yrx,
           qd_s, qd_r, pt_s, pt_r, nu_s, nu_r, wu_s, wu_r, wd_s, wd_r, at_s, at_r,
           c_s, c_r, h_s, h_r, y_s, y_r, loc):
    n_out, reach, steps, q_cnt, heads, hs = cfg
    rows = q_ref.shape[0]
    pos = lax.axis_index("tm")
    head = lax.axis_index("head")
    o, b = pos // 2, pos % 2
    hi, lo = head // 2, head % 2
    partner = pos + 1 - 2 * b
    core = head + 1 - 2 * lo
    cross = lax.rem(head + 2, 4)
    has_up = o + 1 < n_out
    has_dn = o >= 1

    loads = [pltpu.make_async_copy(src, dst, loc.at[i]) for i, (src, dst) in enumerate(
        [(w_hbm, wg.at[o]), (q_hbm, q_ref), (k_hbm, k_ref), (v_hbm, v_ref)])]
    for c in loads:
        c.start()

    barrier = pltpu.get_barrier_semaphore()
    pl.semaphore_signal(barrier, inc=1, device_id={"tm": partner}, device_id_type=MESH)
    pl.semaphore_signal(barrier, inc=1, device_id={"head": core}, device_id_type=MESH)
    pl.semaphore_signal(barrier, inc=1, device_id={"head": cross}, device_id_type=MESH)

    @pl.when(has_up)
    def _():
        pl.semaphore_signal(barrier, inc=1, device_id={"tm": pos + 2}, device_id_type=MESH)

    @pl.when(has_dn)
    def _():
        pl.semaphore_signal(barrier, inc=1, device_id={"tm": pos - 2}, device_id_type=MESH)

    amount = 3 + has_up.astype(jnp.int32) + has_dn.astype(jnp.int32)
    pl.semaphore_wait(barrier, amount)

    def rcopy(src, dst, s, r, axis, index):
        return pltpu.make_async_remote_copy(
            src_ref=src, dst_ref=dst, send_sem=s, recv_sem=r,
            device_id={axis: index}, device_id_type=MESH)

    def q_at(s):
        return q_ref if s == 0 else qd.at[s - 1]

    def q_dn(s):
        return [rcopy(q_at(s - 1), q_at(s), qd_s.at[s - 1], qd_r.at[s - 1], "tm", pos - 2)]

    def n_up(s):
        return [rcopy(ntx.at[s - 1], nrx.at[s - 1], nu_s.at[s - 1, 0], nu_r.at[s - 1, 0],
                      "tm", pos + 2),
                rcopy(dtx.at[s - 1], drx.at[s - 1], nu_s.at[s - 1, 1], nu_r.at[s - 1, 1],
                      "tm", pos + 2)]

    pair_kv = [rcopy(k_ref, kb, pt_s.at[0], pt_r.at[0], "tm", partner),
               rcopy(v_ref, vb, pt_s.at[1], pt_r.at[1], "tm", partner)]

    def w_up(t):
        origin = jnp.maximum(o - t + 1, 0)
        return rcopy(wg.at[origin], wg.at[origin], wu_s.at[t - 1], wu_r.at[t - 1], "tm", pos + 2)

    def w_dn(t):
        origin = jnp.minimum(o + t - 1, n_out - 1)
        return rcopy(wg.at[origin], wg.at[origin], wd_s.at[t - 1], wd_r.at[t - 1], "tm", pos - 2)

    def start_all(cond, copies):
        @pl.when(cond)
        def _():
            for c in copies:
                c.start()

    def wait_recv(cond, copies):
        @pl.when(cond)
        def _():
            for c in copies:
                c.wait_recv()

    def wait_send(cond, copies):
        @pl.when(cond)
        def _():
            for c in copies:
                c.wait_send()

    def up_sends(t):
        return has_up & (o - t + 1 >= 0)

    def dn_sends(t):
        return has_dn & (o + t - 1 < n_out)

    def q_sends(s):
        return has_dn & (o + s - 1 < n_out)

    def n_sends(s):
        return has_up & (o + s < n_out)

    def n_gets(s):
        return has_dn & (o + s < n_out)

    scale = 1.0 / math.sqrt(hs)
    lane = lax.broadcasted_iota(jnp.int32, (rows, 128), 1)

    def attend(s, key_ref, value_ref, slot, first):
        query_ref = q_at(s)
        mask = jnp.concatenate(
            [jnp.broadcast_to(mask_ref[slot, f:f + 1, :], (FRAME, rows))
             for f in range(rows // FRAME)], axis=0)
        if first:
            den[s] = jnp.zeros((rows, 128), jnp.float32)

        def one(h, carry):
            at = pl.ds(pl.multiple_of(h * hs, hs), hs)
            scores = lax.dot_general(query_ref[:, at], key_ref[:, at], (((1,), (1,)), ((), ())),
                                     preferred_element_type=jnp.float32)
            probs = jnp.exp(scores * scale) * mask
            total = jnp.sum(probs, axis=1, keepdims=True)
            part = jnp.dot(probs.astype(jnp.bfloat16), value_ref[:, at],
                           preferred_element_type=jnp.float32)
            den[s] += jnp.where(lane == h, total, 0.0)
            if first:
                num[s, :, at] = part
            else:
                num[s, :, at] += part
            return carry

        lax.fori_loop(0, heads, one, 0)

    def rotate(ref, row):
        gain = gain_ref[row:row + 1, :]
        for h in range(heads):
            at = slice(h * hs, (h + 1) * hs)
            x = ref[:, at].astype(jnp.float32)
            mean_sq = jnp.mean(x * x, axis=1, keepdims=True)
            x = x * lax.rsqrt(mean_sq + 1e-06) * gain
            ref[:, at] = (x * cos_ref[...]
                          + pltpu.roll(x, hs // 2, 1) * sin_ref[...]).astype(jnp.bfloat16)

    loads[0].wait()
    start_all(up_sends(1), [w_up(1)])
    loads[3].wait()
    pair_kv[1].start()
    loads[1].wait()
    rotate(q_ref, 0)
    start_all(q_sends(1), q_dn(1))
    loads[2].wait()
    rotate(k_ref, 1)
    pair_kv[0].start()
    attend(0, k_ref, v_ref, 0, True)

    def down(t):
        wait_recv(o + t < n_out, [w_dn(t)])
        if t + 1 < n_out:
            start_all(dn_sends(t + 1), [w_dn(t + 1)])

    def up(t):
        wait_recv(o - t >= 0, [w_up(t)])
        if t + 1 < n_out:
            start_all(up_sends(t + 1), [w_up(t + 1)])

    for s in range(1, steps + 1):
        wait_recv(o + s < n_out, q_dn(s))
        if s < steps:
            start_all(q_sends(s + 1), q_dn(s + 1))
        if s == max(steps - 1, 1):
            start_all(dn_sends(1), [w_dn(1)])

        @pl.when(o + s < n_out)
        def _():
            attend(s, k_ref, v_ref, 2 * s, True)
        if s == 1:
            up(1)
    for c in pair_kv:
        c.wait_recv()

    def with_pair(s):
        cond = (o + s < n_out) & (((b == 0) & (s >= 1)) | ((b == 1) & (2 * s + 1 <= reach)))

        @pl.when(cond)
        def _():
            attend(s, kb, vb, 2 * s + 1, False)

    def add_up(s):
        if s < steps:
            @pl.when(n_gets(s))
            def _():
                for c in n_up(s + 1):
                    c.wait_recv()
                num[s] += nrx[s].astype(jnp.float32)
                wide = jnp.concatenate(
                    [drx[s], jnp.zeros((120, rows), jnp.float32)], axis=0)
                den[s] += jnp.transpose(wide)
        if s >= 1:
            @pl.when(n_sends(s))
            def _():
                ntx[s - 1] = num[s].astype(jnp.bfloat16)
                dtx[s - 1] = jnp.transpose(den[s])[0:8]
                for c in n_up(s):
                    c.start()

    with_pair(steps)
    add_up(steps)
    for s in range(steps - 1, -1, -1):
        with_pair(s)
    up(2)
    down(1)
    for s in range(steps - 1, -1, -1):
        if s == 0:
            down(2)
        add_up(s)

    for h in range(heads):
        at = slice(h * hs, (h + 1) * hs)
        att[0:rows, at] = (num[0, :, at] / den[0, :, h:h + 1]).astype(jnp.bfloat16)
    swap = rcopy(att.at[pl.ds(0, rows)], att.at[pl.ds(rows, rows)], at_s, at_r, "tm", partner)
    swap.start()
    for t in range(3, n_out):
        down(t)
        up(t)
    swap.wait_recv()

    def project(group, store):
        def one(k, carry):
            weight = jnp.concatenate([wg[group * q_cnt + k, h] for h in range(heads)], axis=1)
            acc = lax.dot_general(att[...], weight, (((1,), (1,)), ((), ())),
                                  preferred_element_type=jnp.float32)
            store(k, acc)
            return carry
        if q_cnt == 1:
            one(0, 0)
        else:
            lax.fori_loop(0, q_cnt, one, 0)

    sides = (1 - hi, hi)
    c_copies = []
    for i, side in enumerate(sides):
        def put(k, acc, i=i):
            ptx[i, k] = acc.astype(jnp.bfloat16)
        project(2 * side + (1 - lo), put)
        copy = rcopy(ptx.at[i], rx1.at[i], c_s.at[i], c_r.at[i], "head", core)
        copy.start()
        c_copies.append(copy)
    for i, side in enumerate(sides):
        def put(k, acc, i=i):
            keep[i, k] = acc
        project(2 * side + lo, put)
    c_copies[0].wait_recv()
    h_copies = [None, None]
    for r in (1, 0):
        at = slice(r * rows, (r + 1) * rows)
        stx[r] = (keep[0, :, at] + rx1[0, :, at].astype(jnp.float32)).astype(jnp.bfloat16)
        h_copies[r] = rcopy(stx.at[r], rx2.at[r], h_s.at[r], h_r.at[r], "head", cross)
        h_copies[r].start()
    c_copies[1].wait_recv()

    def final(r):
        at = slice(r * rows, (r + 1) * rows)
        mine = keep[1, :, at] + rx1[1, :, at].astype(jnp.float32)
        return (mine + rx2[r].astype(jnp.float32)).astype(jnp.bfloat16)

    h_copies[1].wait_recv()
    ytx[...] = final(1)
    y_copy = rcopy(ytx, yrx, y_s, y_r, "tm", partner)
    y_copy.start()
    h_copies[0].wait_recv()
    if len(out_ref.shape) == 2:
        dsl = ytx.shape[-1]
        out_ref[:, pl.ds(pl.multiple_of(b * dsl, 128), dsl)] = final(0)[0]
        y_copy.wait_recv()
        out_ref[:, pl.ds(pl.multiple_of((1 - b) * dsl, 128), dsl)] = yrx[0]
    else:
        out_ref[b] = final(0)
        y_copy.wait_recv()
        out_ref[1 - b] = yrx[...]

    for c in pair_kv:
        c.wait_send()
    for s in range(1, steps + 1):
        wait_send(q_sends(s), q_dn(s))
        wait_send(n_sends(s), n_up(s))
    for t in range(1, n_out):
        wait_send(up_sends(t), [w_up(t)])
        wait_send(dn_sends(t), [w_dn(t)])
    for c in [swap, y_copy] + c_copies + h_copies:
        c.wait_send()


def wide_device(queries, key_input, values, query_gain, key_gain, frames, frame_rate, out_weight):
    rows = queries.shape[0]
    hs = query_gain.shape[0]
    heads = queries.shape[1] // hs
    n = lax.axis_size("tm")
    m = lax.axis_size("head")
    n_out = n // 2
    per = rows // FRAME
    longest = n * per // 2
    back = min(WIN, longest) - 1
    reach = min((back + per - 1) // per, n - 1)
    steps = (reach + 1) // 2
    q_cnt = n_out // m
    dsl = out_weight.shape[1]

    pos = lax.axis_index("tm")
    b = pos % 2
    own_index = pos * rows + jnp.arange(rows, dtype=jnp.int32)
    cosine, sine = rotary(own_index, frames, frame_rate, hs)
    gains = jnp.stack([query_gain, key_gain])

    frames_at = jnp.arange(per, dtype=jnp.int32)
    q_pos = jnp.stack([pos + 2 * (slot // 2) for slot in range(2 * steps + 2)])
    k_pos = jnp.stack([pos, pos + 1 - 2 * b] * (steps + 1))
    q_frame = q_pos[:, None] * per + frames_at[None, :]
    q_clip = clip_of(q_frame.reshape(-1), frames)[0].reshape(q_frame.shape)
    k_frame = (k_pos[:, None] * per
               + (jnp.arange(rows, dtype=jnp.int32) // FRAME)[None, :])
    k_clip = clip_of(k_frame.reshape(-1), frames)[0].reshape(k_frame.shape)
    kf, kc = k_frame[:, None, :], k_clip[:, None, :]
    qf, qc = q_frame[:, :, None], q_clip[:, :, None]
    mask = ((kc == qc) & (kf <= qf) & (kf >= qf - (WIN - 1))).astype(jnp.float32)

    bf, f32 = jnp.bfloat16, jnp.float32
    width = heads * hs
    flat = q_cnt == 1 and dsl % 128 == 0
    shape = (rows, 2 * dsl) if flat else (2, q_cnt, rows, dsl)
    dma = pltpu.SemaphoreType.DMA
    out = pl.pallas_call(
        functools.partial(wide_kernel, (n_out, reach, steps, q_cnt, heads, hs)),
        out_shape=jax.ShapeDtypeStruct(shape, bf),
        in_specs=[pl.BlockSpec(memory_space=pl.ANY)] * 4
        + [pl.BlockSpec(memory_space=pltpu.VMEM)] * 4,
        out_specs=pl.BlockSpec(memory_space=pltpu.VMEM),
        scratch_shapes=[
            pltpu.VMEM((rows, width), bf),
            pltpu.VMEM((rows, width), bf),
            pltpu.VMEM((rows, width), bf),
            pltpu.VMEM((steps, rows, width), bf),
            pltpu.VMEM((rows, width), bf),
            pltpu.VMEM((rows, width), bf),
            pltpu.VMEM((n_out,) + out_weight.shape, bf),
            pltpu.VMEM((steps + 1, rows, width), f32),
            pltpu.VMEM((steps + 1, rows, 128), f32),
            pltpu.VMEM((steps, rows, width), bf),
            pltpu.VMEM((steps, rows, width), bf),
            pltpu.VMEM((steps, 8, rows), f32),
            pltpu.VMEM((steps, 8, rows), f32),
            pltpu.VMEM((2 * rows, width), bf),
            pltpu.VMEM((2, q_cnt, 2 * rows, dsl), bf),
            pltpu.VMEM((2, q_cnt, 2 * rows, dsl), f32),
            pltpu.VMEM((2, q_cnt, 2 * rows, dsl), bf),
            pltpu.VMEM((2, q_cnt, rows, dsl), bf),
            pltpu.VMEM((2, q_cnt, rows, dsl), bf),
            pltpu.VMEM((q_cnt, rows, dsl), bf),
            pltpu.VMEM((q_cnt, rows, dsl), bf),
            dma((steps,)), dma((steps,)), dma((2,)), dma((2,)), dma((steps, 2)), dma((steps, 2)),
            dma((n_out - 1,)), dma((n_out - 1,)), dma((n_out - 1,)), dma((n_out - 1,)),
            dma, dma, dma((2,)), dma((2,)), dma((2,)), dma((2,)), dma, dma, dma((4,)),
        ],
        compiler_params=pltpu.CompilerParams(
            collective_id=0, has_side_effects=True, vmem_limit_bytes=56 * 1024 * 1024
        ),
    )(queries, key_input, values, out_weight, cosine, sine, gains, mask)
    if flat:
        return out
    return jnp.transpose(out, (2, 1, 0, 3)).reshape(rows, 2 * q_cnt * dsl)


def level_kernel(cfg, frames_ref, rate_ref, q_hbm, k_hbm, v_hbm, w_hbm, qg_ref, kg_ref, out_ref,
                 q_in, k_in, cosine, sine, mask_ref, qtx, ktx, qx, kx, vx, num, den,
                 ntx, dtx, nrx, drx, att, far_att, wg, ptx, prx, keep, stx, xrx, ytx, yrx, rtx, rrx,
                 loc, ex_s, ex_r, qd_s, qd_r, kv_s, kv_r, nu_s, nu_r, at_s, at_r, fa_s, fa_r, r_s, r_r,
                 wu_s, wu_r, wd_s, wd_r, c_s, c_r, x_s, x_r, y_s, y_r):
    hs, mine, clips, wide_gap = cfg
    rows = q_in.shape[0]
    level = 2 * rows
    per = level // FRAME
    bf, f32, i32 = jnp.bfloat16, jnp.float32, jnp.int32
    pos = lax.axis_index("tm")
    head = lax.axis_index("head")
    z, y = pos // 2, pos % 2
    x, c = head // 2, head % 2
    partner = {"tm": pos + 1 - 2 * y}
    sibling = {"head": head + 1 - 2 * c}
    cross = {"head": lax.rem(head + 2, 4)}
    above = {"tm": pos + 2}
    below = {"tm": pos - 2}

    def lanes(i, n):
        return pl.ds(pl.multiple_of(i * n, hs), n)

    def half(i, base=0):
        return pl.ds(pl.multiple_of(base + i * rows, rows), rows)

    own_rows, other_rows = half(y), half(1 - y)

    def local(src, dst, i):
        return pltpu.make_async_copy(src, dst, loc.at[i])

    load_q = local(q_hbm, q_in, 0)
    load_k = local(k_hbm, k_in, 1)
    load_w = local(w_hbm, wg.at[z], 2)
    load_v = [local(v_hbm.at[:, lanes(mine * y + h, hs)], vx.at[h, half(y, level)], 3 + h)
              for h in range(mine)]
    for load in [load_q, load_k, load_w] + load_v:
        load.start()

    barrier = pltpu.get_barrier_semaphore()
    for near in (partner, sibling, cross):
        pl.semaphore_signal(barrier, inc=1, device_id=near, device_id_type=MESH)

    @pl.when(z < 3)
    def _():
        pl.semaphore_signal(barrier, inc=1, device_id=above, device_id_type=MESH)

    @pl.when(z > 0)
    def _():
        pl.semaphore_signal(barrier, inc=1, device_id=below, device_id_type=MESH)

    def rcopy(src, dst, s, r, where):
        return pltpu.make_async_remote_copy(
            src_ref=src, dst_ref=dst, send_sem=s, recv_sem=r,
            device_id=where, device_id_type=MESH)

    def q_ex(h):
        return rcopy(qtx.at[h], qx.at[0, h, own_rows], ex_s.at[0, h], ex_r.at[0, h], partner)

    def k_ex(h):
        return rcopy(ktx.at[h], kx.at[h, half(y, level)], ex_s.at[1, h], ex_r.at[1, h], partner)

    def v_ex(h):
        return rcopy(v_hbm.at[:, lanes(mine * (1 - y) + h, hs)], vx.at[h, half(y, level)],
                     ex_s.at[2, h], ex_r.at[2, h], partner)

    def q_dn(i, h):
        at = half(y) if i == 0 else half(1 - y)
        return rcopy(qx.at[0, h, at], qx.at[1, h, at], qd_s.at[i, h], qd_r.at[i, h], below)

    def kv_up(n, h):
        ref, i = (kx, vx)[n % 2], (y, 1 - y)[n // 2]
        return rcopy(ref.at[h, half(i, level)], ref.at[h, half(i)], kv_s.at[n, h], kv_r.at[n, h],
                     above)

    def kv_late(n, h):
        ref, first = (kx, vx)[n % 2], n // 2 == 0
        at, size = (FRAME, rows - FRAME) if first else (rows, rows)
        return rcopy(ref.at[h, pl.ds(level + at, size)], ref.at[h, pl.ds(at, size)],
                     kv_s.at[n, h], kv_r.at[n, h], above)

    def n_up(h):
        return [rcopy(ntx.at[h], nrx.at[h], nu_s.at[0, h], nu_r.at[0, h], above),
                rcopy(dtx.at[h], drx.at[h], nu_s.at[1, h], nu_r.at[1, h], above)]

    def att_dn(h):
        at = mine * y + h
        return rcopy(att.at[at], far_att.at[at], fa_s.at[0, h], fa_r.at[0, h], below)

    def far_swap(h):
        at = far_att.at[mine * y + h]
        return rcopy(at, at, fa_s.at[1, h], fa_r.at[1, h], partner)

    def r_up(j):
        return rcopy(rtx.at[j], rrx.at[j], r_s.at[j], r_r.at[j], above)

    def swap(h):
        at = att.at[mine * y + h]
        return rcopy(at, at, at_s.at[h], at_r.at[h], partner)

    def w_own(j):
        return w_hbm.at[:, pl.ds(j * hs, hs), :]

    def w_piece(o, j):
        return wg.at[o, :, pl.ds(pl.multiple_of(j * hs, hs), hs), :]

    def w_up(o, j, own=False):
        return rcopy(w_own(j) if own else w_piece(o, j), w_piece(o, j), wu_s.at[o, j], wu_r.at[o, j], above)

    def w_dn(o, j, own=False):
        return rcopy(w_own(j) if own else w_piece(o, j), w_piece(o, j), wd_s.at[o, j], wd_r.at[o, j], below)

    pieces = 3

    shape = (2 * 8, hs)
    lane = lax.broadcasted_iota(i32, shape, 1)
    sub = lax.broadcasted_iota(i32, shape, 0)
    pair = jnp.where(lane >= hs // 2, lane - hs // 2, lane)
    side = hs // 6 * 2
    depth = hs - 2 * side
    in_t = pair < depth // 2
    in_h = (pair >= depth // 2) & (pair < depth // 2 + side // 2)
    step = jnp.where(in_t, pair, jnp.where(in_h, pair - depth // 2, pair - depth // 2 - side // 2))
    log = -2.0 * math.log(10000.0)
    freq = jnp.exp(step.astype(f32) * jnp.where(in_t, log / depth, log / side))
    times = []
    for i in range(2):
        frame = 2 * pos + i
        end, start, rate = i32(0), i32(0), i32(0)
        for n in range(clips):
            inside = (frame >= end) & (frame < end + frames_ref[n])
            start = jnp.where(inside, end, start)
            rate = jnp.where(inside, rate_ref[n], rate)
            end = end + frames_ref[n]
        times.append(jnp.full(shape, frame - start, i32).astype(f32) * 24.0
                     / jnp.full(shape, rate, i32).astype(f32))
    sub8 = jnp.where(sub >= 8, sub - 8, sub)
    place = jnp.where(in_t, jnp.where(sub < 8, times[0], times[1]),
                      jnp.where(in_h, sub8, sub).astype(f32))
    angle = place * freq
    cos16 = jnp.cos(angle)
    sin16 = jnp.sin(angle) * jnp.where(lane < hs // 2, -1.0, 1.0)
    for table, small in ((cosine, cos16), (sine, sin16)):
        for i in range(2):
            for r in range(8):
                at = (8 * i + r) * GW
                table[at:at + GW, :] = jnp.where(
                    in_t, jnp.broadcast_to(small[8 * i:8 * i + 1], shape),
                    jnp.where(in_h, jnp.broadcast_to(small[r:r + 1], shape), small))

    def clip_index(frame):
        end, index = i32(0), jnp.zeros(frame.shape, i32)
        for n in range(clips):
            end = end + frames_ref[n]
            index = index + jnp.where(frame >= end, 1, 0)
        return index

    mshape = mask_ref.shape
    q_frame = per * z + lax.broadcasted_iota(i32, mshape, 0)
    k_frame = per * (z - 1) + lax.broadcasted_iota(i32, mshape, 1) // FRAME
    seen = ((clip_index(q_frame) == clip_index(k_frame)) & (k_frame <= q_frame)
            & (k_frame >= q_frame - (WIN - 1)))
    mask_ref[...] = jnp.where(seen, 1.0, 0.0)

    def rotate(src, gain_ref, i, h):
        v = src[:, lanes(mine * i + h, hs)].astype(f32)
        v = v * lax.rsqrt(jnp.mean(v * v, axis=1, keepdims=True) + 1e-06) * gain_ref[...]
        return (v * cosine[...] + pltpu.roll(v, hs // 2, 1) * sine[...]).astype(bf)

    def each(body):
        def step(h, carry):
            body(h)
            return carry
        lax.fori_loop(0, mine, step, 0)

    load_q.wait()
    load_k.wait()
    for load in load_v:
        load.wait()
    amount = 3 + (z < 3).astype(i32) + (z > 0).astype(i32)
    pl.semaphore_wait(barrier, amount)

    @pl.when((z == 2) if wide_gap else ((z == 1) | (z == 2)))
    def _():
        for j in range(2):
            w_up(z, j, True).start()

    @pl.when(z == 1)
    def _():
        for j in range(pieces):
            w_dn(1, j, True).start()

    def spread(h):
        qtx[h] = rotate(q_in, qg_ref, 1 - y, h)
        q_ex(h).start()
        qx[0, h, own_rows, :] = rotate(q_in, qg_ref, y, h)

    def spread_keys(h):
        ktx[h] = rotate(k_in, kg_ref, 1 - y, h)
        k_ex(h).start()
        v_ex(h).start()
        kx[h, half(y, level), :] = rotate(k_in, kg_ref, y, h)

    each(spread)

    @pl.when((z == 3) if wide_gap else (z >= 2))
    def _():
        q_dn(0, 0).start()
    each(spread_keys)
    load_w.wait()

    scale = math.log2(math.e) / math.sqrt(hs)

    def attend(h, slot, block, k0, klen, first, n=rows):
        at = pl.ds(rows * block, n)
        f0 = per * slot + (rows // FRAME) * block
        keys = slice(k0, k0 + klen)
        mask = jnp.concatenate(
            [jnp.broadcast_to(mask_ref[f0 + f:f0 + f + 1, keys], (FRAME, klen))
             for f in range(n // FRAME)], axis=0)
        ones = jnp.ones((klen, hs), bf)
        scores = lax.dot_general(qx[slot, h, at, :], kx[h, keys, :], (((1,), (1,)), ((), ())),
                                 preferred_element_type=f32)
        probs = (jnp.exp2(scores * scale) * mask).astype(bf)
        both = jnp.dot(probs, jnp.concatenate([vx[h, keys, :], ones], axis=1),
                       preferred_element_type=f32)
        if first:
            num[slot, h, at, :] = both[:, :hs]
            den[slot, h, at, :] = both[:, hs:]
        else:
            num[slot, h, at, :] += both[:, :hs]
            den[slot, h, at, :] += both[:, hs:]

    def send_sums(h):
        ntx[h] = num[1, h].astype(bf)
        dtx[h] = jnp.transpose(den[1, h])[0:8]
        for copy in n_up(h):
            copy.start()

    def add_sums(h):
        for copy in n_up(h):
            copy.wait_recv()
        num[0, h] += nrx[h].astype(f32)
        den[0, h] += jnp.transpose(jnp.concatenate([drx[h]] * (hs // 8), axis=0))

    def finish(h):
        att[mine * y + h] = (num[0, h] / den[0, h]).astype(bf)
        swap(h).start()

    def take_up(o, j):
        w_up(o, j).wait_recv()

        @pl.when(z < 3)
        def _():
            w_up(o, j).start()

    def take_dn(o, j):
        w_dn(o, j).wait_recv()

        @pl.when(z > 0)
        def _():
            w_dn(o, j).start()

    def own(h, waits=True):
        if waits:
            q_ex(h).wait_recv()
        attend(h, 0, 0, level, rows, True)
        attend(h, 0, 1, level, level, True)

    def own_below(h):
        attend(h, 0, 0, 0, level, False)
        attend(h, 0, 1, 0, level, False)

    def keys_here(h):
        k_ex(h).wait_recv()
        v_ex(h).wait_recv()

    def queries_here(h):
        q_dn(0, h).wait_recv()
        q_dn(1, h).wait_recv()

    def queries_down():
        for h in range(mine):
            q_ex(h).wait_recv()
            q_dn(1, h).start()
            if h + 1 < mine:
                q_dn(0, h + 1).start()

    @pl.when(z == 0)
    def _():
        kv_up(0, 0).start()
        kv_up(1, 0).start()
        for h in range(mine):
            if h + 1 < mine:
                kv_up(0, h + 1).start()
                kv_up(1, h + 1).start()
            k_ex(h).wait_recv()
            kv_up(2, h).start()
            v_ex(h).wait_recv()
            kv_up(3, h).start()
        for j in range(pieces):
            w_up(0, j, True).start()

        def rest(h):
            own(h)
            finish(h)

        each(rest)

    @pl.when(z == 1)
    def _():
        if wide_gap:
            for i in range(2):
                @pl.when(y == i)
                def _():
                    for h in range(mine):
                        kv_late(2 * i, h).start()
                        kv_late(2 * i + 1, h).start()
            for h in range(mine):
                for n, copy in ((0, k_ex), (1, v_ex)):
                    copy(h).wait_recv()
                    for i in range(2):
                        @pl.when(y != i)
                        def _():
                            kv_late(2 * i + n, h).start()
            for j in range(pieces):
                w_up(1, j, True).start()
            each(own)
        else:
            for h in range(mine):
                keys_here(h)
                queries_here(h)
                attend(h, 1, 0, level, level, True)
                attend(h, 1, 1, level, level, True)
                for n in range(4):
                    kv_up(n, h).wait_recv()
                attend(h, 1, 0, 0, level, False)
                attend(h, 1, 1, rows, rows, False)
                send_sums(h)
            w_up(1, 2, True).start()
            each(own)

        def rest(h):
            if wide_gap:
                for n in range(4):
                    kv_up(n, h).wait_recv()
            own_below(h)
            finish(h)
            take_dn(2, h)

        each(rest)
        for j in range(2):
            take_up(0, j)

    @pl.when(z == 2)
    def _():
        if not wide_gap:
            queries_down()
        for j in range(pieces):
            w_dn(2, j, True).start()

        def above_sums(h):
            keys_here(h)
            queries_here(h)
            attend(h, 1, 0, level, level, True)
            attend(h, 1, 1, level, level, True)
            if wide_gap:
                for n in range(4):
                    kv_late(n, h).wait_recv()
                attend(h, 1, 0, FRAME, level - FRAME, False)
                attend(h, 1, 1, rows, rows, False)
            send_sums(h)

        def rest(h):
            if wide_gap:
                own(h)
                attend(h, 0, 0, FRAME, level - FRAME, False)
                attend(h, 0, 1, FRAME, level - FRAME, False)
            else:
                add_sums(h)
            finish(h)
            if not wide_gap:
                att_dn(h).wait_recv()
                far_swap(h).start()

        each(above_sums)
        w_up(2, 2, True).start()
        if not wide_gap:
            for j in range(2):
                take_up(1, j)
            each(lambda h: own(h, False))
        for j in range(2):
            take_dn(3, j)
        each(rest)

    @pl.when(z == 3)
    def _():
        queries_down()
        for j in range(2):
            w_dn(3, j, True).start()

        def here(h):
            keys_here(h)
            own(h, False)

        def last(h):
            add_sums(h)
            finish(h)
            att_dn(h).start()

        each(here)
        each(last)
        w_dn(3, 2, True).start()

    for h in range(mine):
        swap(h).wait_recv()

    def order(n):
        t, j = n // pieces, n % pieces
        from_one = jnp.where(t == 0, 1, jnp.where(t == 1, 2, jnp.where(t == 2, 0, 3)))
        low = jnp.where((z == 1) | (z == 2), from_one, t)
        o = jnp.where(z < 2, low, 3 - low)
        both = (z == 2) & (n >= 2 * pieces)
        late = n - 2 * pieces
        extra = both & (late % 3 == 0)
        o = jnp.where(both, jnp.where(late % 3 == 1, 3, 0), o)
        j = jnp.where(both, late // 3, j)
        return o, j, extra

    count = jnp.where(z == 2, 5 * pieces, jnp.where(z == 3, 3 * pieces, 4 * pieces))

    def sum_at(o, j, extra):
        return jnp.where(extra, 2 * pieces, (o // 2) * pieces) + j

    def to_sibling(m):
        return rcopy(ptx.at[m], prx.at[m], c_s.at[m], c_r.at[m], sibling)

    def to_cross(i):
        return rcopy(stx.at[i], xrx.at[i], x_s.at[i], x_r.at[i], cross)

    def to_partner(j):
        return rcopy(ytx.at[j], yrx.at[j], y_s.at[j], y_r.at[j], partner)

    def result(j):
        m = (head // 2) * pieces + j
        to_cross(j).wait_recv()
        ytx[j] = (keep[m, other_rows, :] + xrx[j, other_rows, :].astype(f32)).astype(bf)
        to_partner(j).start()
        out_ref[:, lanes(pieces * y + j, hs)] = (
            keep[m, own_rows, :] + xrx[j, own_rows, :].astype(f32)).astype(bf)

    def far_sum(j):
        r_up(j).wait_recv()

        @pl.when(x == 0)
        def _():
            keep[j] = rrx[j].astype(f32)

        @pl.when(x == 1)
        def _():
            stx[j] = rrx[j]
            to_cross(j).start()

    def project(n, carry):
        @pl.when((z == 1) & (n < 3 * pieces) & (n % 3 == 0))
        def _():
            @pl.when(n == 0)
            def _():
                take_up(0, 2)

            take_dn(3, n // 3)

        if wide_gap:
            @pl.when((z == 2) & (n < pieces))
            def _():
                take_up(1, n)
        else:
            @pl.when((z == 2) & (n == 0))
            def _():
                take_up(1, 2)

        if wide_gap:
            @pl.when((z == 2) & (n == 0))
            def _():
                for h in range(mine):
                    att_dn(h).wait_recv()
                    far_swap(h).start()

        @pl.when((z == 2) & (n == pieces))
        def _():
            take_dn(3, 2)

        @pl.when((z == 2) & (n == 2 * pieces))
        def _():
            for h in range(mine):
                far_swap(h).wait_recv()

        @pl.when(n < count)
        def _():
            o, j, extra = order(n)

            @pl.when((z == 0) & (o > 0))
            def _():
                w_dn(o, j).wait_recv()

            @pl.when((z == 3) & (o < 3))
            def _():
                w_up(o, j).wait_recv()

            @pl.when(extra)
            def _():
                w_up(0, j).wait_recv()

            weight = jnp.concatenate(
                [wg[o, h, pl.ds(pl.multiple_of(j * hs, hs), hs), :] for h in range(2 * mine)], axis=1)
            m = sum_at(o, j, extra)

            def spread_sum(held):
                rows_in = jnp.concatenate([held[h] for h in range(2 * mine)], axis=1)
                acc = lax.dot_general(rows_in, weight, (((1,), (1,)), ((), ())),
                                      preferred_element_type=f32)

                @pl.when(o % 2 != c)
                def _():
                    ptx[m] = acc.astype(bf)
                    to_sibling(m).start()

                @pl.when(o % 2 == c)
                def _():
                    keep[m] = acc

            @pl.when(extra)
            def _():
                spread_sum(far_att)

            @pl.when(~extra)
            def _():
                spread_sum(att)

        o1, j1, extra1 = order(n - 2)

        @pl.when((n >= 2) & (n < count + 2) & (o1 % 2 == c))
        def _():
            m = sum_at(o1, j1, extra1)
            to_sibling(m).wait_recv()

            @pl.when(extra1)
            def _():
                rtx[j1] = (keep[m] + prx[m].astype(f32)).astype(bf)
                r_up(j1).start()

            @pl.when(~extra1 & (o1 // 2 != x))
            def _():
                stx[j1] = (keep[m] + prx[m].astype(f32)).astype(bf)
                to_cross(j1).start()

            @pl.when(~extra1 & (o1 // 2 == x))
            def _():
                keep[m] = keep[m] + prx[m].astype(f32)

        return carry

    lax.fori_loop(0, count + 2, project, 0)

    bare = (z == 3) & (head == 0)

    @pl.when(~bare)
    def _():
        for j in range(pieces):
            result(j)

    @pl.when((z == 3) & (c == 0))
    def _():
        for j in range(pieces):
            far_sum(j)

    @pl.when(bare)
    def _():
        for j in range(pieces):
            result(j)

    for j in range(pieces):
        to_partner(j).wait_recv()
        out_ref[:, lanes(pieces * (1 - y) + j, hs)] = yrx[j]

    def sent(h):
        for copy in (q_ex(h), k_ex(h), v_ex(h), swap(h)):
            copy.wait_send()

        @pl.when((z == 3) if wide_gap else (z >= 2))
        def _():
            q_dn(0, h).wait_send()
            q_dn(1, h).wait_send()

        @pl.when(z == 0)
        def _():
            for n in range(4):
                kv_up(n, h).wait_send()

        @pl.when((z == 2) if wide_gap else ((z == 1) | (z == 2)))
        def _():
            for copy in n_up(h):
                copy.wait_send()

        if wide_gap:
            @pl.when(z == 1)
            def _():
                for n in range(4):
                    kv_late(n, h).wait_send()

        @pl.when(z == 3)
        def _():
            att_dn(h).wait_send()

        @pl.when(z == 2)
        def _():
            far_swap(h).wait_send()

    each(sent)

    for o in range(4):
        @pl.when(((z == 0) | (z == 1)) if o == 0 else ((z < 3) & (z >= o)))
        def _():
            for j in range(pieces):
                w_up(o, j).wait_send()

        @pl.when((z > 0) & (z <= o))
        def _():
            for j in range(pieces):
                w_dn(o, j).wait_send()

    @pl.when(~((z == 3) & (c == 1)))
    def _():
        for m in range(pieces):
            to_sibling(m).wait_send()
    for m in range(pieces, 2 * pieces):
        to_sibling(m).wait_send()

    @pl.when((z == 2) & (c == 1))
    def _():
        for m in range(2 * pieces, 3 * pieces):
            to_sibling(m).wait_send()

    @pl.when((z == 2) & (c == 0))
    def _():
        for j in range(pieces):
            r_up(j).wait_send()
    for j in range(pieces):
        to_cross(j).wait_send()
        to_partner(j).wait_send()


def level_device(wide_gap, queries, key_input, values, query_gain, key_gain, frames, frame_rate, out_weight):
    rows, width = queries.shape
    hs = query_gain.shape[0]
    mine = width // hs // 2
    level = 2 * rows
    pieces = out_weight.shape[1] // hs
    bf, f32 = jnp.bfloat16, jnp.float32
    dma = pltpu.SemaphoreType.DMA
    vmem = pltpu.VMEM
    smem = pl.BlockSpec(memory_space=pltpu.SMEM)
    near = pl.BlockSpec(memory_space=pltpu.VMEM)
    far = pl.BlockSpec(memory_space=pl.ANY)
    return pl.pallas_call(
        functools.partial(level_kernel, (hs, mine, frames.shape[0], wide_gap)),
        out_shape=jax.ShapeDtypeStruct((rows, width), bf),
        in_specs=[smem, smem, far, far, far, far, near, near],
        out_specs=near,
        scratch_shapes=[
            vmem((rows, width), bf), vmem((rows, width), bf),
            vmem((rows, hs), f32), vmem((rows, hs), f32),
            vmem((16, 2 * level), f32),
            vmem((mine, rows, hs), bf), vmem((mine, rows, hs), bf),
            vmem((2, mine, level, hs), bf),
            vmem((mine, 2 * level, hs), bf), vmem((mine, 2 * level, hs), bf),
            vmem((2, mine, level, hs), f32), vmem((2, mine, level, hs), f32),
            vmem((mine, level, hs), bf), vmem((mine, 8, level), f32),
            vmem((mine, level, hs), bf), vmem((mine, 8, level), f32),
            vmem((2 * mine, level, hs), bf), vmem((2 * mine, level, hs), bf),
            vmem((4,) + out_weight.shape, bf),
            vmem((3 * pieces, level, hs), bf), vmem((3 * pieces, level, hs), bf),
            vmem((3 * pieces, level, hs), f32),
            vmem((pieces, level, hs), bf), vmem((pieces, level, hs), bf),
            vmem((pieces, rows, hs), bf), vmem((pieces, rows, hs), bf),
            vmem((pieces, level, hs), bf), vmem((pieces, level, hs), bf),
            dma((3 + mine,)), dma((3, mine)), dma((3, mine)), dma((2, mine)), dma((2, mine)),
            dma((4, mine)), dma((4, mine)), dma((2, mine)), dma((2, mine)),
            dma((mine,)), dma((mine,)), dma((2, mine)), dma((2, mine)), dma((pieces,)), dma((pieces,)),
            dma((4, pieces)), dma((4, pieces)), dma((4, pieces)), dma((4, pieces)),
            dma((3 * pieces,)), dma((3 * pieces,)), dma((pieces,)), dma((pieces,)),
            dma((pieces,)), dma((pieces,)),
        ],
        compiler_params=pltpu.CompilerParams(
            collective_id=int(wide_gap), has_side_effects=True, vmem_limit_bytes=56 * 1024 * 1024
        ),
    )(frames, frame_rate, queries, key_input, values, out_weight,
      query_gain.reshape(1, hs), key_gain.reshape(1, hs))


def per_device(queries, key_input, values, query_gain, key_gain, frames, frame_rate, out_weight):
    args = (queries, key_input, values, query_gain, key_gain, frames, frame_rate, out_weight)
    rows, width = queries.shape
    heads, columns, hs = out_weight.shape
    fits = (lax.axis_size("tm") == 8 and lax.axis_size("head") == 4 and rows == 2 * FRAME
            and FRAME == 8 * GW and hs == 128 and heads % 2 == 0
            and columns == width // 2 == 3 * hs)
    if fits:
        count = frames.shape[0]
        upto = jnp.arange(count)[:, None] >= jnp.arange(count)[None, :]
        ends = jnp.sum(jnp.where(upto, frames[None, :], 0), axis=1)
        spans = (ends - frames <= 7) & (ends > 12)
        return lax.cond(jnp.any(spans), functools.partial(level_device, True),
                        functools.partial(level_device, False), *args)
    return wide_device(*args)


def solution(mesh):
    in_specs = (
        P("tm", "head"),
        P("tm", "head"),
        P("tm", "head"),
        P(),
        P(),
        P(),
        P(),
        P("head", "tm", None),
    )
    out_specs = P("tm", "head")
    return jax.shard_map(
        per_device, mesh=mesh, in_specs=in_specs, out_specs=out_specs, check_vma=False
    )
```

```python
import functools
import math

import jax
import jax.numpy as jnp
from jax import lax
from jax.experimental import pallas as pl
from jax.experimental.pallas import tpu as pltpu
from jax.sharding import PartitionSpec as P

GW = 16
WIN = 12
FRAME = 128
MESH = pl.DeviceIdType.MESH


def rope_freqs(width):
    steps = jnp.arange(width // 2, dtype=jnp.float32)
    return jnp.exp(steps * (-2.0 * math.log(10000.0) / width))


def clip_of(frame_global, frames):
    count = frames.shape[0]
    upto = jnp.arange(count)[:, None] >= jnp.arange(count)[None, :]
    ends = jnp.sum(jnp.where(upto, frames[None, :], 0), axis=1)
    starts = ends - frames
    inside = (
        (frame_global[:, None] >= starts[None, :]) & (frame_global[:, None] < ends[None, :])
    ).astype(jnp.int32)
    clip_id = jnp.sum(inside * jnp.arange(frames.shape[0], dtype=jnp.int32)[None, :], axis=1)
    return (clip_id, inside, starts)


def rotary(token_index, frames, frame_rate, head_size):
    frame_global = token_index // FRAME
    clip_id, inside, starts = clip_of(frame_global, frames)
    frame_start = jnp.sum(inside * starts[None, :], axis=1)
    rate_token = jnp.sum(inside * frame_rate[None, :], axis=1).astype(jnp.float32)
    in_frame = token_index % FRAME
    time_pos = (frame_global - frame_start).astype(jnp.float32) * 24.0 / rate_token
    row_pos = (in_frame // GW).astype(jnp.float32)
    col_pos = (in_frame % GW).astype(jnp.float32)
    side = head_size // 6 * 2
    depth = head_size - 2 * side
    angles = jnp.concatenate(
        [
            time_pos[:, None] * rope_freqs(depth)[None, :],
            row_pos[:, None] * rope_freqs(side)[None, :],
            col_pos[:, None] * rope_freqs(side)[None, :],
        ],
        axis=1,
    )
    cosine, sine = jnp.cos(angles), jnp.sin(angles)
    return (jnp.concatenate([cosine, cosine], axis=1), jnp.concatenate([-sine, sine], axis=1))


def wide_kernel(cfg, q_hbm, k_hbm, v_hbm, w_hbm, cos_ref, sin_ref, gain_ref, mask_ref, out_ref,
           q_ref, k_ref, v_ref, qd, kb, vb, wg, num, den, ntx, nrx, dtx, drx, att, ptx, keep, rx1, stx, rx2, ytx, yrx,
           qd_s, qd_r, pt_s, pt_r, nu_s, nu_r, wu_s, wu_r, wd_s, wd_r, at_s, at_r,
           c_s, c_r, h_s, h_r, y_s, y_r, loc):
    n_out, reach, steps, q_cnt, heads, hs = cfg
    rows = q_ref.shape[0]
    pos = lax.axis_index("tm")
    head = lax.axis_index("head")
    o, b = pos // 2, pos % 2
    hi, lo = head // 2, head % 2
    partner = pos + 1 - 2 * b
    core = head + 1 - 2 * lo
    cross = lax.rem(head + 2, 4)
    has_up = o + 1 < n_out
    has_dn = o >= 1

    loads = [pltpu.make_async_copy(src, dst, loc.at[i]) for i, (src, dst) in enumerate(
        [(w_hbm, wg.at[o]), (q_hbm, q_ref), (k_hbm, k_ref), (v_hbm, v_ref)])]
    for c in loads:
        c.start()

    barrier = pltpu.get_barrier_semaphore()
    pl.semaphore_signal(barrier, inc=1, device_id={"tm": partner}, device_id_type=MESH)
    pl.semaphore_signal(barrier, inc=1, device_id={"head": core}, device_id_type=MESH)
    pl.semaphore_signal(barrier, inc=1, device_id={"head": cross}, device_id_type=MESH)

    @pl.when(has_up)
    def _():
        pl.semaphore_signal(barrier, inc=1, device_id={"tm": pos + 2}, device_id_type=MESH)

    @pl.when(has_dn)
    def _():
        pl.semaphore_signal(barrier, inc=1, device_id={"tm": pos - 2}, device_id_type=MESH)

    amount = 3 + has_up.astype(jnp.int32) + has_dn.astype(jnp.int32)
    pl.semaphore_wait(barrier, amount)

    def rcopy(src, dst, s, r, axis, index):
        return pltpu.make_async_remote_copy(
            src_ref=src, dst_ref=dst, send_sem=s, recv_sem=r,
            device_id={axis: index}, device_id_type=MESH)

    def q_at(s):
        return q_ref if s == 0 else qd.at[s - 1]

    def q_dn(s):
        return [rcopy(q_at(s - 1), q_at(s), qd_s.at[s - 1], qd_r.at[s - 1], "tm", pos - 2)]

    def n_up(s):
        return [rcopy(ntx.at[s - 1], nrx.at[s - 1], nu_s.at[s - 1, 0], nu_r.at[s - 1, 0],
                      "tm", pos + 2),
                rcopy(dtx.at[s - 1], drx.at[s - 1], nu_s.at[s - 1, 1], nu_r.at[s - 1, 1],
                      "tm", pos + 2)]

    pair_kv = [rcopy(k_ref, kb, pt_s.at[0], pt_r.at[0], "tm", partner),
               rcopy(v_ref, vb, pt_s.at[1], pt_r.at[1], "tm", partner)]

    def w_up(t):
        origin = jnp.maximum(o - t + 1, 0)
        return rcopy(wg.at[origin], wg.at[origin], wu_s.at[t - 1], wu_r.at[t - 1], "tm", pos + 2)

    def w_dn(t):
        origin = jnp.minimum(o + t - 1, n_out - 1)
        return rcopy(wg.at[origin], wg.at[origin], wd_s.at[t - 1], wd_r.at[t - 1], "tm", pos - 2)

    def start_all(cond, copies):
        @pl.when(cond)
        def _():
            for c in copies:
                c.start()

    def wait_recv(cond, copies):
        @pl.when(cond)
        def _():
            for c in copies:
                c.wait_recv()

    def wait_send(cond, copies):
        @pl.when(cond)
        def _():
            for c in copies:
                c.wait_send()

    def up_sends(t):
        return has_up & (o - t + 1 >= 0)

    def dn_sends(t):
        return has_dn & (o + t - 1 < n_out)

    def q_sends(s):
        return has_dn & (o + s - 1 < n_out)

    def n_sends(s):
        return has_up & (o + s < n_out)

    def n_gets(s):
        return has_dn & (o + s < n_out)

    scale = 1.0 / math.sqrt(hs)
    lane = lax.broadcasted_iota(jnp.int32, (rows, 128), 1)

    def attend(s, key_ref, value_ref, slot, first):
        query_ref = q_at(s)
        mask = jnp.concatenate(
            [jnp.broadcast_to(mask_ref[slot, f:f + 1, :], (FRAME, rows))
             for f in range(rows // FRAME)], axis=0)
        if first:
            den[s] = jnp.zeros((rows, 128), jnp.float32)

        def one(h, carry):
            at = pl.ds(pl.multiple_of(h * hs, hs), hs)
            scores = lax.dot_general(query_ref[:, at], key_ref[:, at], (((1,), (1,)), ((), ())),
                                     preferred_element_type=jnp.float32)
            probs = jnp.exp(scores * scale) * mask
            total = jnp.sum(probs, axis=1, keepdims=True)
            part = jnp.dot(probs.astype(jnp.bfloat16), value_ref[:, at],
                           preferred_element_type=jnp.float32)
            den[s] += jnp.where(lane == h, total, 0.0)
            if first:
                num[s, :, at] = part
            else:
                num[s, :, at] += part
            return carry

        lax.fori_loop(0, heads, one, 0)

    def rotate(ref, row):
        gain = gain_ref[row:row + 1, :]
        for h in range(heads):
            at = slice(h * hs, (h + 1) * hs)
            x = ref[:, at].astype(jnp.float32)
            mean_sq = jnp.mean(x * x, axis=1, keepdims=True)
            x = x * lax.rsqrt(mean_sq + 1e-06) * gain
            ref[:, at] = (x * cos_ref[...]
                          + pltpu.roll(x, hs // 2, 1) * sin_ref[...]).astype(jnp.bfloat16)

    loads[0].wait()
    start_all(up_sends(1), [w_up(1)])
    loads[3].wait()
    pair_kv[1].start()
    loads[1].wait()
    rotate(q_ref, 0)
    start_all(q_sends(1), q_dn(1))
    loads[2].wait()
    rotate(k_ref, 1)
    pair_kv[0].start()
    attend(0, k_ref, v_ref, 0, True)

    def down(t):
        wait_recv(o + t < n_out, [w_dn(t)])
        if t + 1 < n_out:
            start_all(dn_sends(t + 1), [w_dn(t + 1)])

    def up(t):
        wait_recv(o - t >= 0, [w_up(t)])
        if t + 1 < n_out:
            start_all(up_sends(t + 1), [w_up(t + 1)])

    for s in range(1, steps + 1):
        wait_recv(o + s < n_out, q_dn(s))
        if s < steps:
            start_all(q_sends(s + 1), q_dn(s + 1))
        if s == max(steps - 1, 1):
            start_all(dn_sends(1), [w_dn(1)])

        @pl.when(o + s < n_out)
        def _():
            attend(s, k_ref, v_ref, 2 * s, True)
        if s == 1:
            up(1)
    for c in pair_kv:
        c.wait_recv()

    def with_pair(s):
        cond = (o + s < n_out) & (((b == 0) & (s >= 1)) | ((b == 1) & (2 * s + 1 <= reach)))

        @pl.when(cond)
        def _():
            attend(s, kb, vb, 2 * s + 1, False)

    def add_up(s):
        if s < steps:
            @pl.when(n_gets(s))
            def _():
                for c in n_up(s + 1):
                    c.wait_recv()
                num[s] += nrx[s].astype(jnp.float32)
                wide = jnp.concatenate(
                    [drx[s], jnp.zeros((120, rows), jnp.float32)], axis=0)
                den[s] += jnp.transpose(wide)
        if s >= 1:
            @pl.when(n_sends(s))
            def _():
                ntx[s - 1] = num[s].astype(jnp.bfloat16)
                dtx[s - 1] = jnp.transpose(den[s])[0:8]
                for c in n_up(s):
                    c.start()

    with_pair(steps)
    add_up(steps)
    for s in range(steps - 1, -1, -1):
        with_pair(s)
    up(2)
    down(1)
    for s in range(steps - 1, -1, -1):
        if s == 0:
            down(2)
        add_up(s)

    for h in range(heads):
        at = slice(h * hs, (h + 1) * hs)
        att[0:rows, at] = (num[0, :, at] / den[0, :, h:h + 1]).astype(jnp.bfloat16)
    swap = rcopy(att.at[pl.ds(0, rows)], att.at[pl.ds(rows, rows)], at_s, at_r, "tm", partner)
    swap.start()
    for t in range(3, n_out):
        down(t)
        up(t)
    swap.wait_recv()

    def project(group, store):
        def one(k, carry):
            weight = jnp.concatenate([wg[group * q_cnt + k, h] for h in range(heads)], axis=1)
            acc = lax.dot_general(att[...], weight, (((1,), (1,)), ((), ())),
                                  preferred_element_type=jnp.float32)
            store(k, acc)
            return carry
        if q_cnt == 1:
            one(0, 0)
        else:
            lax.fori_loop(0, q_cnt, one, 0)

    sides = (1 - hi, hi)
    c_copies = []
    for i, side in enumerate(sides):
        def put(k, acc, i=i):
            ptx[i, k] = acc.astype(jnp.bfloat16)
        project(2 * side + (1 - lo), put)
        copy = rcopy(ptx.at[i], rx1.at[i], c_s.at[i], c_r.at[i], "head", core)
        copy.start()
        c_copies.append(copy)
    for i, side in enumerate(sides):
        def put(k, acc, i=i):
            keep[i, k] = acc
        project(2 * side + lo, put)
    c_copies[0].wait_recv()
    h_copies = [None, None]
    for r in (1, 0):
        at = slice(r * rows, (r + 1) * rows)
        stx[r] = (keep[0, :, at] + rx1[0, :, at].astype(jnp.float32)).astype(jnp.bfloat16)
        h_copies[r] = rcopy(stx.at[r], rx2.at[r], h_s.at[r], h_r.at[r], "head", cross)
        h_copies[r].start()
    c_copies[1].wait_recv()

    def final(r):
        at = slice(r * rows, (r + 1) * rows)
        mine = keep[1, :, at] + rx1[1, :, at].astype(jnp.float32)
        return (mine + rx2[r].astype(jnp.float32)).astype(jnp.bfloat16)

    h_copies[1].wait_recv()
    ytx[...] = final(1)
    y_copy = rcopy(ytx, yrx, y_s, y_r, "tm", partner)
    y_copy.start()
    h_copies[0].wait_recv()
    if len(out_ref.shape) == 2:
        dsl = ytx.shape[-1]
        out_ref[:, pl.ds(pl.multiple_of(b * dsl, 128), dsl)] = final(0)[0]
        y_copy.wait_recv()
        out_ref[:, pl.ds(pl.multiple_of((1 - b) * dsl, 128), dsl)] = yrx[0]
    else:
        out_ref[b] = final(0)
        y_copy.wait_recv()
        out_ref[1 - b] = yrx[...]

    for c in pair_kv:
        c.wait_send()
    for s in range(1, steps + 1):
        wait_send(q_sends(s), q_dn(s))
        wait_send(n_sends(s), n_up(s))
    for t in range(1, n_out):
        wait_send(up_sends(t), [w_up(t)])
        wait_send(dn_sends(t), [w_dn(t)])
    for c in [swap, y_copy] + c_copies + h_copies:
        c.wait_send()


def wide_device(queries, key_input, values, query_gain, key_gain, frames, frame_rate, out_weight):
    rows = queries.shape[0]
    hs = query_gain.shape[0]
    heads = queries.shape[1] // hs
    n = lax.axis_size("tm")
    m = lax.axis_size("head")
    n_out = n // 2
    per = rows // FRAME
    longest = n * per // 2
    back = min(WIN, longest) - 1
    reach = min((back + per - 1) // per, n - 1)
    steps = (reach + 1) // 2
    q_cnt = n_out // m
    dsl = out_weight.shape[1]

    pos = lax.axis_index("tm")
    b = pos % 2
    own_index = pos * rows + jnp.arange(rows, dtype=jnp.int32)
    cosine, sine = rotary(own_index, frames, frame_rate, hs)
    gains = jnp.stack([query_gain, key_gain])

    frames_at = jnp.arange(per, dtype=jnp.int32)
    q_pos = jnp.stack([pos + 2 * (slot // 2) for slot in range(2 * steps + 2)])
    k_pos = jnp.stack([pos, pos + 1 - 2 * b] * (steps + 1))
    q_frame = q_pos[:, None] * per + frames_at[None, :]
    q_clip = clip_of(q_frame.reshape(-1), frames)[0].reshape(q_frame.shape)
    k_frame = (k_pos[:, None] * per
               + (jnp.arange(rows, dtype=jnp.int32) // FRAME)[None, :])
    k_clip = clip_of(k_frame.reshape(-1), frames)[0].reshape(k_frame.shape)
    kf, kc = k_frame[:, None, :], k_clip[:, None, :]
    qf, qc = q_frame[:, :, None], q_clip[:, :, None]
    mask = ((kc == qc) & (kf <= qf) & (kf >= qf - (WIN - 1))).astype(jnp.float32)

    bf, f32 = jnp.bfloat16, jnp.float32
    width = heads * hs
    flat = q_cnt == 1 and dsl % 128 == 0
    shape = (rows, 2 * dsl) if flat else (2, q_cnt, rows, dsl)
    dma = pltpu.SemaphoreType.DMA
    out = pl.pallas_call(
        functools.partial(wide_kernel, (n_out, reach, steps, q_cnt, heads, hs)),
        out_shape=jax.ShapeDtypeStruct(shape, bf),
        in_specs=[pl.BlockSpec(memory_space=pl.ANY)] * 4
        + [pl.BlockSpec(memory_space=pltpu.VMEM)] * 4,
        out_specs=pl.BlockSpec(memory_space=pltpu.VMEM),
        scratch_shapes=[
            pltpu.VMEM((rows, width), bf),
            pltpu.VMEM((rows, width), bf),
            pltpu.VMEM((rows, width), bf),
            pltpu.VMEM((steps, rows, width), bf),
            pltpu.VMEM((rows, width), bf),
            pltpu.VMEM((rows, width), bf),
            pltpu.VMEM((n_out,) + out_weight.shape, bf),
            pltpu.VMEM((steps + 1, rows, width), f32),
            pltpu.VMEM((steps + 1, rows, 128), f32),
            pltpu.VMEM((steps, rows, width), bf),
            pltpu.VMEM((steps, rows, width), bf),
            pltpu.VMEM((steps, 8, rows), f32),
            pltpu.VMEM((steps, 8, rows), f32),
            pltpu.VMEM((2 * rows, width), bf),
            pltpu.VMEM((2, q_cnt, 2 * rows, dsl), bf),
            pltpu.VMEM((2, q_cnt, 2 * rows, dsl), f32),
            pltpu.VMEM((2, q_cnt, 2 * rows, dsl), bf),
            pltpu.VMEM((2, q_cnt, rows, dsl), bf),
            pltpu.VMEM((2, q_cnt, rows, dsl), bf),
            pltpu.VMEM((q_cnt, rows, dsl), bf),
            pltpu.VMEM((q_cnt, rows, dsl), bf),
            dma((steps,)), dma((steps,)), dma((2,)), dma((2,)), dma((steps, 2)), dma((steps, 2)),
            dma((n_out - 1,)), dma((n_out - 1,)), dma((n_out - 1,)), dma((n_out - 1,)),
            dma, dma, dma((2,)), dma((2,)), dma((2,)), dma((2,)), dma, dma, dma((4,)),
        ],
        compiler_params=pltpu.CompilerParams(
            collective_id=0, has_side_effects=True, vmem_limit_bytes=56 * 1024 * 1024
        ),
    )(queries, key_input, values, out_weight, cosine, sine, gains, mask)
    if flat:
        return out
    return jnp.transpose(out, (2, 1, 0, 3)).reshape(rows, 2 * q_cnt * dsl)


def level_kernel(cfg, frames_ref, rate_ref, q_hbm, k_hbm, v_hbm, w_hbm, qg_ref, kg_ref, out_ref,
                 q_in, k_in, cosine, sine, mask_ref, qtx, ktx, qx, kx, vx, num, den,
                 ntx, dtx, nrx, drx, att, far_att, wg, ptx, prx, keep, stx, xrx, ytx, yrx, rtx, rrx,
                 loc, ex_s, ex_r, qd_s, qd_r, kv_s, kv_r, nu_s, nu_r, at_s, at_r, fa_s, fa_r, r_s, r_r,
                 wu_s, wu_r, wd_s, wd_r, c_s, c_r, x_s, x_r, y_s, y_r):
    hs, mine, clips, wide_gap = cfg
    rows = q_in.shape[0]
    level = 2 * rows
    per = level // FRAME
    bf, f32, i32 = jnp.bfloat16, jnp.float32, jnp.int32
    pos = lax.axis_index("tm")
    head = lax.axis_index("head")
    z, y = pos // 2, pos % 2
    x, c = head // 2, head % 2
    partner = {"tm": pos + 1 - 2 * y}
    sibling = {"head": head + 1 - 2 * c}
    cross = {"head": lax.rem(head + 2, 4)}
    above = {"tm": pos + 2}
    below = {"tm": pos - 2}

    def lanes(i, n):
        return pl.ds(pl.multiple_of(i * n, hs), n)

    def half(i, base=0):
        return pl.ds(pl.multiple_of(base + i * rows, rows), rows)

    own_rows, other_rows = half(y), half(1 - y)

    def local(src, dst, i):
        return pltpu.make_async_copy(src, dst, loc.at[i])

    load_q = local(q_hbm, q_in, 0)
    load_k = local(k_hbm, k_in, 1)
    load_w = local(w_hbm, wg.at[z], 2)
    load_v = [local(v_hbm.at[:, lanes(mine * y + h, hs)], vx.at[h, half(y, level)], 3 + h)
              for h in range(mine)]
    for load in [load_q, load_k, load_w] + load_v:
        load.start()

    barrier = pltpu.get_barrier_semaphore()
    for near in (partner, sibling, cross):
        pl.semaphore_signal(barrier, inc=1, device_id=near, device_id_type=MESH)

    @pl.when(z < 3)
    def _():
        pl.semaphore_signal(barrier, inc=1, device_id=above, device_id_type=MESH)

    @pl.when(z > 0)
    def _():
        pl.semaphore_signal(barrier, inc=1, device_id=below, device_id_type=MESH)

    def rcopy(src, dst, s, r, where):
        return pltpu.make_async_remote_copy(
            src_ref=src, dst_ref=dst, send_sem=s, recv_sem=r,
            device_id=where, device_id_type=MESH)

    def q_ex(h):
        return rcopy(qtx.at[h], qx.at[0, h, own_rows], ex_s.at[0, h], ex_r.at[0, h], partner)

    def k_ex(h):
        return rcopy(ktx.at[h], kx.at[h, half(y, level)], ex_s.at[1, h], ex_r.at[1, h], partner)

    def v_ex(h):
        return rcopy(v_hbm.at[:, lanes(mine * (1 - y) + h, hs)], vx.at[h, half(y, level)],
                     ex_s.at[2, h], ex_r.at[2, h], partner)

    def q_dn(i, h):
        at = half(y) if i == 0 else half(1 - y)
        return rcopy(qx.at[0, h, at], qx.at[1, h, at], qd_s.at[i, h], qd_r.at[i, h], below)

    def kv_up(n, h):
        ref, i = (kx, vx)[n % 2], (y, 1 - y)[n // 2]
        return rcopy(ref.at[h, half(i, level)], ref.at[h, half(i)], kv_s.at[n, h], kv_r.at[n, h],
                     above)

    def kv_late(n, h):
        ref, first = (kx, vx)[n % 2], n // 2 == 0
        at, size = (FRAME, rows - FRAME) if first else (rows, rows)
        return rcopy(ref.at[h, pl.ds(level + at, size)], ref.at[h, pl.ds(at, size)],
                     kv_s.at[n, h], kv_r.at[n, h], above)

    def n_up(h):
        return [rcopy(ntx.at[h], nrx.at[h], nu_s.at[0, h], nu_r.at[0, h], above),
                rcopy(dtx.at[h], drx.at[h], nu_s.at[1, h], nu_r.at[1, h], above)]

    def att_dn(h):
        at = mine * y + h
        return rcopy(att.at[at], far_att.at[at], fa_s.at[0, h], fa_r.at[0, h], below)

    def far_swap(h):
        at = far_att.at[mine * y + h]
        return rcopy(at, at, fa_s.at[1, h], fa_r.at[1, h], partner)

    def r_up(j):
        return rcopy(rtx.at[j], rrx.at[j], r_s.at[j], r_r.at[j], above)

    def swap(h):
        at = att.at[mine * y + h]
        return rcopy(at, at, at_s.at[h], at_r.at[h], partner)

    def w_own(j):
        return w_hbm.at[:, pl.ds(j * hs, hs), :]

    def w_piece(o, j):
        return wg.at[o, :, pl.ds(pl.multiple_of(j * hs, hs), hs), :]

    def w_up(o, j, own=False):
        return rcopy(w_own(j) if own else w_piece(o, j), w_piece(o, j), wu_s.at[o, j], wu_r.at[o, j], above)

    def w_dn(o, j, own=False):
        return rcopy(w_own(j) if own else w_piece(o, j), w_piece(o, j), wd_s.at[o, j], wd_r.at[o, j], below)

    pieces = 3

    shape = (2 * 8, hs)
    lane = lax.broadcasted_iota(i32, shape, 1)
    sub = lax.broadcasted_iota(i32, shape, 0)
    pair = jnp.where(lane >= hs // 2, lane - hs // 2, lane)
    side = hs // 6 * 2
    depth = hs - 2 * side
    in_t = pair < depth // 2
    in_h = (pair >= depth // 2) & (pair < depth // 2 + side // 2)
    step = jnp.where(in_t, pair, jnp.where(in_h, pair - depth // 2, pair - depth // 2 - side // 2))
    log = -2.0 * math.log(10000.0)
    freq = jnp.exp(step.astype(f32) * jnp.where(in_t, log / depth, log / side))
    times = []
    for i in range(2):
        frame = 2 * pos + i
        end, start, rate = i32(0), i32(0), i32(0)
        for n in range(clips):
            inside = (frame >= end) & (frame < end + frames_ref[n])
            start = jnp.where(inside, end, start)
            rate = jnp.where(inside, rate_ref[n], rate)
            end = end + frames_ref[n]
        times.append(jnp.full(shape, frame - start, i32).astype(f32) * 24.0
                     / jnp.full(shape, rate, i32).astype(f32))
    sub8 = jnp.where(sub >= 8, sub - 8, sub)
    place = jnp.where(in_t, jnp.where(sub < 8, times[0], times[1]),
                      jnp.where(in_h, sub8, sub).astype(f32))
    angle = place * freq
    cos16 = jnp.cos(angle)
    sin16 = jnp.sin(angle) * jnp.where(lane < hs // 2, -1.0, 1.0)
    for table, small in ((cosine, cos16), (sine, sin16)):
        for i in range(2):
            for r in range(8):
                at = (8 * i + r) * GW
                table[at:at + GW, :] = jnp.where(
                    in_t, jnp.broadcast_to(small[8 * i:8 * i + 1], shape),
                    jnp.where(in_h, jnp.broadcast_to(small[r:r + 1], shape), small))

    def clip_index(frame):
        end, index = i32(0), jnp.zeros(frame.shape, i32)
        for n in range(clips):
            end = end + frames_ref[n]
            index = index + jnp.where(frame >= end, 1, 0)
        return index

    mshape = mask_ref.shape
    q_frame = per * z + lax.broadcasted_iota(i32, mshape, 0)
    k_frame = per * (z - 1) + lax.broadcasted_iota(i32, mshape, 1) // FRAME
    seen = ((clip_index(q_frame) == clip_index(k_frame)) & (k_frame <= q_frame)
            & (k_frame >= q_frame - (WIN - 1)))
    mask_ref[...] = jnp.where(seen, 1.0, 0.0)

    def rotate(src, gain_ref, i, h):
        v = src[:, lanes(mine * i + h, hs)].astype(f32)
        v = v * lax.rsqrt(jnp.mean(v * v, axis=1, keepdims=True) + 1e-06) * gain_ref[...]
        return (v * cosine[...] + pltpu.roll(v, hs // 2, 1) * sine[...]).astype(bf)

    def each(body):
        def step(h, carry):
            body(h)
            return carry
        lax.fori_loop(0, mine, step, 0)

    load_q.wait()
    load_k.wait()
    for load in load_v:
        load.wait()
    amount = 3 + (z < 3).astype(i32) + (z > 0).astype(i32)
    pl.semaphore_wait(barrier, amount)

    @pl.when((z == 2) if wide_gap else ((z == 1) | (z == 2)))
    def _():
        for j in range(2):
            w_up(z, j, True).start()

    @pl.when(z == 1)
    def _():
        for j in range(pieces):
            w_dn(1, j, True).start()

    def spread(h):
        qtx[h] = rotate(q_in, qg_ref, 1 - y, h)
        q_ex(h).start()
        qx[0, h, own_rows, :] = rotate(q_in, qg_ref, y, h)

        @pl.when((z == 3) if wide_gap else (z >= 2))
        def _():
            q_dn(0, h).start()

    def spread_keys(h):
        v_ex(h).start()
        ktx[h] = rotate(k_in, kg_ref, 1 - y, h)
        k_ex(h).start()
        kx[h, half(y, level), :] = rotate(k_in, kg_ref, y, h)

        @pl.when((z == 0) & (h == 0))
        def _():
            kv_up(0, 0).start()
            kv_up(1, 0).start()

    keys_first = z < 3 if wide_gap else z < 2

    @pl.when(keys_first)
    def _():
        each(spread_keys)

    each(spread)

    @pl.when(~keys_first)
    def _():
        each(spread_keys)

    load_w.wait()

    scale = math.log2(math.e) / math.sqrt(hs)

    def attend(h, slot, block, k0, klen, first, n=rows):
        at = pl.ds(rows * block, n)
        f0 = per * slot + (rows // FRAME) * block
        keys = slice(k0, k0 + klen)
        mask = jnp.concatenate(
            [jnp.broadcast_to(mask_ref[f0 + f:f0 + f + 1, keys], (FRAME, klen))
             for f in range(n // FRAME)], axis=0)
        ones = jnp.ones((klen, hs), bf)
        scores = lax.dot_general(qx[slot, h, at, :], kx[h, keys, :], (((1,), (1,)), ((), ())),
                                 preferred_element_type=f32)
        probs = (jnp.exp2(scores * scale) * mask).astype(bf)
        both = jnp.dot(probs, jnp.concatenate([vx[h, keys, :], ones], axis=1),
                       preferred_element_type=f32)
        if first:
            num[slot, h, at, :] = both[:, :hs]
            den[slot, h, at, :] = both[:, hs:]
        else:
            num[slot, h, at, :] += both[:, :hs]
            den[slot, h, at, :] += both[:, hs:]

    def send_sums(h):
        ntx[h] = num[1, h].astype(bf)
        dtx[h] = jnp.transpose(den[1, h])[0:8]
        for copy in n_up(h):
            copy.start()

    def add_sums(h):
        for copy in n_up(h):
            copy.wait_recv()
        num[0, h] += nrx[h].astype(f32)
        den[0, h] += jnp.transpose(jnp.concatenate([drx[h]] * (hs // 8), axis=0))

    def finish(h):
        att[mine * y + h] = (num[0, h] / den[0, h]).astype(bf)
        swap(h).start()

    def take_up(o, j):
        w_up(o, j).wait_recv()

        @pl.when(z < 3)
        def _():
            w_up(o, j).start()

    def take_dn(o, j):
        w_dn(o, j).wait_recv()

        @pl.when(z > 0)
        def _():
            w_dn(o, j).start()

    def own(h, waits=True):
        if waits:
            q_ex(h).wait_recv()
        attend(h, 0, 0, level, rows, True)
        attend(h, 0, 1, level, level, True)

    def own_below(h):
        attend(h, 0, 0, 0, level, False)
        attend(h, 0, 1, 0, level, False)

    def keys_here(h):
        k_ex(h).wait_recv()
        v_ex(h).wait_recv()

    def queries_here(h):
        q_dn(0, h).wait_recv()
        q_dn(1, h).wait_recv()

    def queries_down():
        for h in range(mine):
            q_ex(h).wait_recv()
            q_dn(1, h).start()

    def take_far():
        for h in range(mine):
            if h == 2:
                take_dn(3, 2)
            att_dn(h).wait_recv()
            far_swap(h).start()

    @pl.when(z == 0)
    def _():
        for h in range(mine):
            if h + 1 < mine:
                kv_up(0, h + 1).start()
                kv_up(1, h + 1).start()
            k_ex(h).wait_recv()
            kv_up(2, h).start()
            v_ex(h).wait_recv()
            kv_up(3, h).start()
        for j in range(pieces):
            w_up(0, j, True).start()

        def rest(h):
            own(h)
            finish(h)

        each(rest)

    @pl.when(z == 1)
    def _():
        if wide_gap:
            for i in range(2):
                @pl.when(y == i)
                def _():
                    for h in range(mine):
                        kv_late(2 * i, h).start()
                        kv_late(2 * i + 1, h).start()
            for h in range(mine):
                for n, copy in ((0, k_ex), (1, v_ex)):
                    copy(h).wait_recv()
                    for i in range(2):
                        @pl.when(y != i)
                        def _():
                            kv_late(2 * i + n, h).start()
            for j in range(pieces):
                w_up(1, j, True).start()
            for j in range(2):
                take_dn(2, j)
            each(own)
        else:
            for h in range(mine):
                keys_here(h)
                queries_here(h)
                attend(h, 1, 0, level, level, True)
                attend(h, 1, 1, level, level, True)
                for n in range(4):
                    kv_up(n, h).wait_recv()
                attend(h, 1, 0, 0, level, False)
                attend(h, 1, 1, rows, rows, False)
                send_sums(h)
                if h == 0:
                    w_up(1, 2, True).start()
                else:
                    take_dn(2, h - 1)
            each(own)

        def rest(h):
            if wide_gap:
                for n in range(4):
                    kv_up(n, h).wait_recv()
            own_below(h)
            finish(h)

        take_dn(2, 2)
        each(rest)
        take_up(0, 0)
        take_dn(3, 0)
        take_up(0, 1)

    @pl.when(z == 2)
    def _():
        if not wide_gap:
            queries_down()
        for j in range(pieces):
            w_dn(2, j, True).start()

        def above_sums(h):
            keys_here(h)
            queries_here(h)
            attend(h, 1, 0, level, level, True)
            attend(h, 1, 1, level, level, True)
            if wide_gap:
                for n in range(4):
                    kv_late(n, h).wait_recv()
                attend(h, 1, 0, FRAME, level - FRAME, False)
                attend(h, 1, 1, rows, rows, False)
            send_sums(h)

        def rest(h):
            if wide_gap:
                own(h)
                attend(h, 0, 0, FRAME, level - FRAME, False)
                attend(h, 0, 1, FRAME, level - FRAME, False)
            else:
                add_sums(h)
            finish(h)

        each(above_sums)
        w_up(2, 2, True).start()
        if not wide_gap:
            for j in range(2):
                take_up(1, j)
            each(lambda h: own(h, False))
        for j in range(2):
            take_dn(3, j)
        each(rest)
        if not wide_gap:
            take_far()

    @pl.when(z == 3)
    def _():
        queries_down()
        for j in range(2):
            w_dn(3, j, True).start()

        def here(h):
            keys_here(h)
            own(h, False)

        def last(h):
            add_sums(h)
            finish(h)
            att_dn(h).start()

        each(here)
        for h in range(mine):
            if h == 2:
                w_dn(3, 2, True).start()
            last(h)

    for h in range(mine):
        swap(h).wait_recv()

    def order(n):
        t, j = n // pieces, n % pieces
        from_one = jnp.where(t == 0, 1, jnp.where(t == 1, 2, jnp.where(t == 2, 0, 3)))
        low = jnp.where((z == 1) | (z == 2), from_one, t)
        o = jnp.where(z < 2, low, 3 - low)
        both = (z == 2) & (n >= 2 * pieces)
        late = n - 2 * pieces
        extra = both & (late % 3 == 0)
        o = jnp.where(both, jnp.where(late % 3 == 1, 3, 0), o)
        j = jnp.where(both, late // 3, j)
        return o, j, extra

    count = jnp.where(z == 2, 5 * pieces, jnp.where(z == 3, 3 * pieces, 4 * pieces))

    def sum_at(o, j, extra):
        return jnp.where(extra, 2 * pieces, (o // 2) * pieces) + j

    def to_sibling(m):
        return rcopy(ptx.at[m], prx.at[m], c_s.at[m], c_r.at[m], sibling)

    def to_cross(i):
        return rcopy(stx.at[i], xrx.at[i], x_s.at[i], x_r.at[i], cross)

    def to_partner(j):
        return rcopy(ytx.at[j], yrx.at[j], y_s.at[j], y_r.at[j], partner)

    def result(j):
        m = (head // 2) * pieces + j
        to_cross(j).wait_recv()
        ytx[j] = (keep[m, other_rows, :] + xrx[j, other_rows, :].astype(f32)).astype(bf)
        to_partner(j).start()
        out_ref[:, lanes(pieces * y + j, hs)] = (
            keep[m, own_rows, :] + xrx[j, own_rows, :].astype(f32)).astype(bf)

    def far_sum(j):
        r_up(j).wait_recv()

        @pl.when(x == 0)
        def _():
            keep[j] = rrx[j].astype(f32)

        @pl.when(x == 1)
        def _():
            stx[j] = rrx[j]
            to_cross(j).start()

    lag = jnp.where(z == 0, 1, jnp.where(z == 2, 2, 3))

    def project(n, carry):
        o1, j1, extra1 = order(n - lag)

        @pl.when((n >= lag) & (n < count + lag) & (o1 % 2 == c))
        def _():
            m = sum_at(o1, j1, extra1)
            to_sibling(m).wait_recv()

            @pl.when(extra1)
            def _():
                rtx[j1] = (keep[m] + prx[m].astype(f32)).astype(bf)
                r_up(j1).start()

            @pl.when(~extra1 & (o1 // 2 != x))
            def _():
                stx[j1] = (keep[m] + prx[m].astype(f32)).astype(bf)
                to_cross(j1).start()

            @pl.when(~extra1 & (o1 // 2 == x))
            def _():
                keep[m] = keep[m] + prx[m].astype(f32)

        @pl.when((z == 1) & (n == 2))
        def _():
            take_up(0, 2)

        @pl.when((z == 1) & (n == 1))
        def _():
            take_dn(3, 1)

        @pl.when((z == 1) & (n == 6))
        def _():
            take_dn(3, 2)

        if wide_gap:
            @pl.when((z == 2) & (n < pieces))
            def _():
                take_up(1, n)
        else:
            @pl.when((z == 2) & (n == 0))
            def _():
                take_up(1, 2)

        if wide_gap:
            @pl.when((z == 2) & (n == pieces))
            def _():
                take_far()

        @pl.when((z == 2) & (n == 2 * pieces))
        def _():
            for h in range(mine):
                far_swap(h).wait_recv()

        @pl.when(n < count)
        def _():
            o, j, extra = order(n)

            @pl.when((z == 0) & (o > 0))
            def _():
                w_dn(o, j).wait_recv()

            @pl.when((z == 3) & (o < 3))
            def _():
                w_up(o, j).wait_recv()

            @pl.when(extra)
            def _():
                w_up(0, j).wait_recv()

            weight = jnp.concatenate(
                [wg[o, h, pl.ds(pl.multiple_of(j * hs, hs), hs), :] for h in range(2 * mine)], axis=1)
            m = sum_at(o, j, extra)

            def spread_sum(held):
                rows_in = jnp.concatenate([held[h] for h in range(2 * mine)], axis=1)
                acc = lax.dot_general(rows_in, weight, (((1,), (1,)), ((), ())),
                                      preferred_element_type=f32)

                @pl.when(o % 2 != c)
                def _():
                    ptx[m] = acc.astype(bf)
                    to_sibling(m).start()

                @pl.when(o % 2 == c)
                def _():
                    keep[m] = acc

            @pl.when(extra)
            def _():
                spread_sum(far_att)

            @pl.when(~extra)
            def _():
                spread_sum(att)

        return carry

    lax.fori_loop(0, count + lag, project, 0)

    bare = (z == 3) & (head == 0)

    @pl.when(~bare)
    def _():
        for j in range(pieces):
            result(j)

    @pl.when((z == 3) & (c == 0))
    def _():
        for j in range(pieces):
            far_sum(j)

    @pl.when(bare)
    def _():
        for j in range(pieces):
            result(j)

    for j in range(pieces):
        to_partner(j).wait_recv()
        out_ref[:, lanes(pieces * (1 - y) + j, hs)] = yrx[j]

    def sent(h):
        for copy in (q_ex(h), k_ex(h), v_ex(h), swap(h)):
            copy.wait_send()

        @pl.when((z == 3) if wide_gap else (z >= 2))
        def _():
            q_dn(0, h).wait_send()
            q_dn(1, h).wait_send()

        @pl.when(z == 0)
        def _():
            for n in range(4):
                kv_up(n, h).wait_send()

        @pl.when((z == 2) if wide_gap else ((z == 1) | (z == 2)))
        def _():
            for copy in n_up(h):
                copy.wait_send()

        if wide_gap:
            @pl.when(z == 1)
            def _():
                for n in range(4):
                    kv_late(n, h).wait_send()

        @pl.when(z == 3)
        def _():
            att_dn(h).wait_send()

        @pl.when(z == 2)
        def _():
            far_swap(h).wait_send()

    each(sent)

    for o in range(4):
        @pl.when(((z == 0) | (z == 1)) if o == 0 else ((z < 3) & (z >= o)))
        def _():
            for j in range(pieces):
                w_up(o, j).wait_send()

        @pl.when((z > 0) & (z <= o))
        def _():
            for j in range(pieces):
                w_dn(o, j).wait_send()

    @pl.when(~((z == 3) & (c == 1)))
    def _():
        for m in range(pieces):
            to_sibling(m).wait_send()
    for m in range(pieces, 2 * pieces):
        to_sibling(m).wait_send()

    @pl.when((z == 2) & (c == 1))
    def _():
        for m in range(2 * pieces, 3 * pieces):
            to_sibling(m).wait_send()

    @pl.when((z == 2) & (c == 0))
    def _():
        for j in range(pieces):
            r_up(j).wait_send()
    for j in range(pieces):
        to_cross(j).wait_send()
        to_partner(j).wait_send()


def level_device(wide_gap, queries, key_input, values, query_gain, key_gain, frames, frame_rate, out_weight):
    rows, width = queries.shape
    hs = query_gain.shape[0]
    mine = width // hs // 2
    level = 2 * rows
    pieces = out_weight.shape[1] // hs
    bf, f32 = jnp.bfloat16, jnp.float32
    dma = pltpu.SemaphoreType.DMA
    vmem = pltpu.VMEM
    smem = pl.BlockSpec(memory_space=pltpu.SMEM)
    near = pl.BlockSpec(memory_space=pltpu.VMEM)
    far = pl.BlockSpec(memory_space=pl.ANY)
    return pl.pallas_call(
        functools.partial(level_kernel, (hs, mine, frames.shape[0], wide_gap)),
        out_shape=jax.ShapeDtypeStruct((rows, width), bf),
        in_specs=[smem, smem, far, far, far, far, near, near],
        out_specs=near,
        scratch_shapes=[
            vmem((rows, width), bf), vmem((rows, width), bf),
            vmem((rows, hs), f32), vmem((rows, hs), f32),
            vmem((16, 2 * level), f32),
            vmem((mine, rows, hs), bf), vmem((mine, rows, hs), bf),
            vmem((2, mine, level, hs), bf),
            vmem((mine, 2 * level, hs), bf), vmem((mine, 2 * level, hs), bf),
            vmem((2, mine, level, hs), f32), vmem((2, mine, level, hs), f32),
            vmem((mine, level, hs), bf), vmem((mine, 8, level), f32),
            vmem((mine, level, hs), bf), vmem((mine, 8, level), f32),
            vmem((2 * mine, level, hs), bf), vmem((2 * mine, level, hs), bf),
            vmem((4,) + out_weight.shape, bf),
            vmem((3 * pieces, level, hs), bf), vmem((3 * pieces, level, hs), bf),
            vmem((3 * pieces, level, hs), f32),
            vmem((pieces, level, hs), bf), vmem((pieces, level, hs), bf),
            vmem((pieces, rows, hs), bf), vmem((pieces, rows, hs), bf),
            vmem((pieces, level, hs), bf), vmem((pieces, level, hs), bf),
            dma((3 + mine,)), dma((3, mine)), dma((3, mine)), dma((2, mine)), dma((2, mine)),
            dma((4, mine)), dma((4, mine)), dma((2, mine)), dma((2, mine)),
            dma((mine,)), dma((mine,)), dma((2, mine)), dma((2, mine)), dma((pieces,)), dma((pieces,)),
            dma((4, pieces)), dma((4, pieces)), dma((4, pieces)), dma((4, pieces)),
            dma((3 * pieces,)), dma((3 * pieces,)), dma((pieces,)), dma((pieces,)),
            dma((pieces,)), dma((pieces,)),
        ],
        compiler_params=pltpu.CompilerParams(
            collective_id=int(wide_gap), has_side_effects=True, vmem_limit_bytes=56 * 1024 * 1024
        ),
    )(frames, frame_rate, queries, key_input, values, out_weight,
      query_gain.reshape(1, hs), key_gain.reshape(1, hs))


def per_device(queries, key_input, values, query_gain, key_gain, frames, frame_rate, out_weight):
    args = (queries, key_input, values, query_gain, key_gain, frames, frame_rate, out_weight)
    rows, width = queries.shape
    heads, columns, hs = out_weight.shape
    fits = (lax.axis_size("tm") == 8 and lax.axis_size("head") == 4 and rows == 2 * FRAME
            and FRAME == 8 * GW and hs == 128 and heads % 2 == 0
            and columns == width // 2 == 3 * hs)
    if fits:
        count = frames.shape[0]
        upto = jnp.arange(count)[:, None] >= jnp.arange(count)[None, :]
        ends = jnp.sum(jnp.where(upto, frames[None, :], 0), axis=1)
        spans = (ends - frames <= 7) & (ends > 12)
        return lax.cond(jnp.any(spans), functools.partial(level_device, True),
                        functools.partial(level_device, False), *args)
    return wide_device(*args)


def solution(mesh):
    in_specs = (
        P("tm", "head"),
        P("tm", "head"),
        P("tm", "head"),
        P(),
        P(),
        P(),
        P(),
        P("head", "tm", None),
    )
    out_specs = P("tm", "head")
    return jax.shard_map(
        per_device, mesh=mesh, in_specs=in_specs, out_specs=out_specs, check_vma=False
    )
```

```python
import functools
import math

import jax
import jax.numpy as jnp
from jax import lax
from jax.experimental import pallas as pl
from jax.experimental.pallas import tpu as pltpu
from jax.sharding import PartitionSpec as P

GW = 16
WIN = 12
FRAME = 128
MESH = pl.DeviceIdType.MESH


def rope_freqs(width):
    steps = jnp.arange(width // 2, dtype=jnp.float32)
    return jnp.exp(steps * (-2.0 * math.log(10000.0) / width))


def clip_of(frame_global, frames):
    count = frames.shape[0]
    upto = jnp.arange(count)[:, None] >= jnp.arange(count)[None, :]
    ends = jnp.sum(jnp.where(upto, frames[None, :], 0), axis=1)
    starts = ends - frames
    inside = (
        (frame_global[:, None] >= starts[None, :]) & (frame_global[:, None] < ends[None, :])
    ).astype(jnp.int32)
    clip_id = jnp.sum(inside * jnp.arange(frames.shape[0], dtype=jnp.int32)[None, :], axis=1)
    return (clip_id, inside, starts)


def rotary(token_index, frames, frame_rate, head_size):
    frame_global = token_index // FRAME
    clip_id, inside, starts = clip_of(frame_global, frames)
    frame_start = jnp.sum(inside * starts[None, :], axis=1)
    rate_token = jnp.sum(inside * frame_rate[None, :], axis=1).astype(jnp.float32)
    in_frame = token_index % FRAME
    time_pos = (frame_global - frame_start).astype(jnp.float32) * 24.0 / rate_token
    row_pos = (in_frame // GW).astype(jnp.float32)
    col_pos = (in_frame % GW).astype(jnp.float32)
    side = head_size // 6 * 2
    depth = head_size - 2 * side
    angles = jnp.concatenate(
        [
            time_pos[:, None] * rope_freqs(depth)[None, :],
            row_pos[:, None] * rope_freqs(side)[None, :],
            col_pos[:, None] * rope_freqs(side)[None, :],
        ],
        axis=1,
    )
    cosine, sine = jnp.cos(angles), jnp.sin(angles)
    return (jnp.concatenate([cosine, cosine], axis=1), jnp.concatenate([-sine, sine], axis=1))


def wide_kernel(cfg, q_hbm, k_hbm, v_hbm, w_hbm, cos_ref, sin_ref, gain_ref, mask_ref, out_ref,
           q_ref, k_ref, v_ref, qd, kb, vb, wg, num, den, ntx, nrx, dtx, drx, att, ptx, keep, rx1, stx, rx2, ytx, yrx,
           qd_s, qd_r, pt_s, pt_r, nu_s, nu_r, wu_s, wu_r, wd_s, wd_r, at_s, at_r,
           c_s, c_r, h_s, h_r, y_s, y_r, loc):
    n_out, reach, steps, q_cnt, heads, hs = cfg
    rows = q_ref.shape[0]
    pos = lax.axis_index("tm")
    head = lax.axis_index("head")
    o, b = pos // 2, pos % 2
    hi, lo = head // 2, head % 2
    partner = pos + 1 - 2 * b
    core = head + 1 - 2 * lo
    cross = lax.rem(head + 2, 4)
    has_up = o + 1 < n_out
    has_dn = o >= 1

    loads = [pltpu.make_async_copy(src, dst, loc.at[i]) for i, (src, dst) in enumerate(
        [(w_hbm, wg.at[o]), (q_hbm, q_ref), (k_hbm, k_ref), (v_hbm, v_ref)])]
    for c in loads:
        c.start()

    barrier = pltpu.get_barrier_semaphore()
    pl.semaphore_signal(barrier, inc=1, device_id={"tm": partner}, device_id_type=MESH)
    pl.semaphore_signal(barrier, inc=1, device_id={"head": core}, device_id_type=MESH)
    pl.semaphore_signal(barrier, inc=1, device_id={"head": cross}, device_id_type=MESH)

    @pl.when(has_up)
    def _():
        pl.semaphore_signal(barrier, inc=1, device_id={"tm": pos + 2}, device_id_type=MESH)

    @pl.when(has_dn)
    def _():
        pl.semaphore_signal(barrier, inc=1, device_id={"tm": pos - 2}, device_id_type=MESH)

    amount = 3 + has_up.astype(jnp.int32) + has_dn.astype(jnp.int32)
    pl.semaphore_wait(barrier, amount)

    def rcopy(src, dst, s, r, axis, index):
        return pltpu.make_async_remote_copy(
            src_ref=src, dst_ref=dst, send_sem=s, recv_sem=r,
            device_id={axis: index}, device_id_type=MESH)

    def q_at(s):
        return q_ref if s == 0 else qd.at[s - 1]

    def q_dn(s):
        return [rcopy(q_at(s - 1), q_at(s), qd_s.at[s - 1], qd_r.at[s - 1], "tm", pos - 2)]

    def n_up(s):
        return [rcopy(ntx.at[s - 1], nrx.at[s - 1], nu_s.at[s - 1, 0], nu_r.at[s - 1, 0],
                      "tm", pos + 2),
                rcopy(dtx.at[s - 1], drx.at[s - 1], nu_s.at[s - 1, 1], nu_r.at[s - 1, 1],
                      "tm", pos + 2)]

    pair_kv = [rcopy(k_ref, kb, pt_s.at[0], pt_r.at[0], "tm", partner),
               rcopy(v_ref, vb, pt_s.at[1], pt_r.at[1], "tm", partner)]

    def w_up(t):
        origin = jnp.maximum(o - t + 1, 0)
        return rcopy(wg.at[origin], wg.at[origin], wu_s.at[t - 1], wu_r.at[t - 1], "tm", pos + 2)

    def w_dn(t):
        origin = jnp.minimum(o + t - 1, n_out - 1)
        return rcopy(wg.at[origin], wg.at[origin], wd_s.at[t - 1], wd_r.at[t - 1], "tm", pos - 2)

    def start_all(cond, copies):
        @pl.when(cond)
        def _():
            for c in copies:
                c.start()

    def wait_recv(cond, copies):
        @pl.when(cond)
        def _():
            for c in copies:
                c.wait_recv()

    def wait_send(cond, copies):
        @pl.when(cond)
        def _():
            for c in copies:
                c.wait_send()

    def up_sends(t):
        return has_up & (o - t + 1 >= 0)

    def dn_sends(t):
        return has_dn & (o + t - 1 < n_out)

    def q_sends(s):
        return has_dn & (o + s - 1 < n_out)

    def n_sends(s):
        return has_up & (o + s < n_out)

    def n_gets(s):
        return has_dn & (o + s < n_out)

    scale = 1.0 / math.sqrt(hs)
    lane = lax.broadcasted_iota(jnp.int32, (rows, 128), 1)

    def attend(s, key_ref, value_ref, slot, first):
        query_ref = q_at(s)
        mask = jnp.concatenate(
            [jnp.broadcast_to(mask_ref[slot, f:f + 1, :], (FRAME, rows))
             for f in range(rows // FRAME)], axis=0)
        if first:
            den[s] = jnp.zeros((rows, 128), jnp.float32)

        def one(h, carry):
            at = pl.ds(pl.multiple_of(h * hs, hs), hs)
            scores = lax.dot_general(query_ref[:, at], key_ref[:, at], (((1,), (1,)), ((), ())),
                                     preferred_element_type=jnp.float32)
            probs = jnp.exp(scores * scale) * mask
            total = jnp.sum(probs, axis=1, keepdims=True)
            part = jnp.dot(probs.astype(jnp.bfloat16), value_ref[:, at],
                           preferred_element_type=jnp.float32)
            den[s] += jnp.where(lane == h, total, 0.0)
            if first:
                num[s, :, at] = part
            else:
                num[s, :, at] += part
            return carry

        lax.fori_loop(0, heads, one, 0)

    def rotate(ref, row):
        gain = gain_ref[row:row + 1, :]
        for h in range(heads):
            at = slice(h * hs, (h + 1) * hs)
            x = ref[:, at].astype(jnp.float32)
            mean_sq = jnp.mean(x * x, axis=1, keepdims=True)
            x = x * lax.rsqrt(mean_sq + 1e-06) * gain
            ref[:, at] = (x * cos_ref[...]
                          + pltpu.roll(x, hs // 2, 1) * sin_ref[...]).astype(jnp.bfloat16)

    loads[0].wait()
    start_all(up_sends(1), [w_up(1)])
    loads[3].wait()
    pair_kv[1].start()
    loads[1].wait()
    rotate(q_ref, 0)
    start_all(q_sends(1), q_dn(1))
    loads[2].wait()
    rotate(k_ref, 1)
    pair_kv[0].start()
    attend(0, k_ref, v_ref, 0, True)

    def down(t):
        wait_recv(o + t < n_out, [w_dn(t)])
        if t + 1 < n_out:
            start_all(dn_sends(t + 1), [w_dn(t + 1)])

    def up(t):
        wait_recv(o - t >= 0, [w_up(t)])
        if t + 1 < n_out:
            start_all(up_sends(t + 1), [w_up(t + 1)])

    for s in range(1, steps + 1):
        wait_recv(o + s < n_out, q_dn(s))
        if s < steps:
            start_all(q_sends(s + 1), q_dn(s + 1))
        if s == max(steps - 1, 1):
            start_all(dn_sends(1), [w_dn(1)])

        @pl.when(o + s < n_out)
        def _():
            attend(s, k_ref, v_ref, 2 * s, True)
        if s == 1:
            up(1)
    for c in pair_kv:
        c.wait_recv()

    def with_pair(s):
        cond = (o + s < n_out) & (((b == 0) & (s >= 1)) | ((b == 1) & (2 * s + 1 <= reach)))

        @pl.when(cond)
        def _():
            attend(s, kb, vb, 2 * s + 1, False)

    def add_up(s):
        if s < steps:
            @pl.when(n_gets(s))
            def _():
                for c in n_up(s + 1):
                    c.wait_recv()
                num[s] += nrx[s].astype(jnp.float32)
                wide = jnp.concatenate(
                    [drx[s], jnp.zeros((120, rows), jnp.float32)], axis=0)
                den[s] += jnp.transpose(wide)
        if s >= 1:
            @pl.when(n_sends(s))
            def _():
                ntx[s - 1] = num[s].astype(jnp.bfloat16)
                dtx[s - 1] = jnp.transpose(den[s])[0:8]
                for c in n_up(s):
                    c.start()

    with_pair(steps)
    add_up(steps)
    for s in range(steps - 1, -1, -1):
        with_pair(s)
    up(2)
    down(1)
    for s in range(steps - 1, -1, -1):
        if s == 0:
            down(2)
        add_up(s)

    for h in range(heads):
        at = slice(h * hs, (h + 1) * hs)
        att[0:rows, at] = (num[0, :, at] / den[0, :, h:h + 1]).astype(jnp.bfloat16)
    swap = rcopy(att.at[pl.ds(0, rows)], att.at[pl.ds(rows, rows)], at_s, at_r, "tm", partner)
    swap.start()
    for t in range(3, n_out):
        down(t)
        up(t)
    swap.wait_recv()

    def project(group, store):
        def one(k, carry):
            weight = jnp.concatenate([wg[group * q_cnt + k, h] for h in range(heads)], axis=1)
            acc = lax.dot_general(att[...], weight, (((1,), (1,)), ((), ())),
                                  preferred_element_type=jnp.float32)
            store(k, acc)
            return carry
        if q_cnt == 1:
            one(0, 0)
        else:
            lax.fori_loop(0, q_cnt, one, 0)

    sides = (1 - hi, hi)
    c_copies = []
    for i, side in enumerate(sides):
        def put(k, acc, i=i):
            ptx[i, k] = acc.astype(jnp.bfloat16)
        project(2 * side + (1 - lo), put)
        copy = rcopy(ptx.at[i], rx1.at[i], c_s.at[i], c_r.at[i], "head", core)
        copy.start()
        c_copies.append(copy)
    for i, side in enumerate(sides):
        def put(k, acc, i=i):
            keep[i, k] = acc
        project(2 * side + lo, put)
    c_copies[0].wait_recv()
    h_copies = [None, None]
    for r in (1, 0):
        at = slice(r * rows, (r + 1) * rows)
        stx[r] = (keep[0, :, at] + rx1[0, :, at].astype(jnp.float32)).astype(jnp.bfloat16)
        h_copies[r] = rcopy(stx.at[r], rx2.at[r], h_s.at[r], h_r.at[r], "head", cross)
        h_copies[r].start()
    c_copies[1].wait_recv()

    def final(r):
        at = slice(r * rows, (r + 1) * rows)
        mine = keep[1, :, at] + rx1[1, :, at].astype(jnp.float32)
        return (mine + rx2[r].astype(jnp.float32)).astype(jnp.bfloat16)

    h_copies[1].wait_recv()
    ytx[...] = final(1)
    y_copy = rcopy(ytx, yrx, y_s, y_r, "tm", partner)
    y_copy.start()
    h_copies[0].wait_recv()
    if len(out_ref.shape) == 2:
        dsl = ytx.shape[-1]
        out_ref[:, pl.ds(pl.multiple_of(b * dsl, 128), dsl)] = final(0)[0]
        y_copy.wait_recv()
        out_ref[:, pl.ds(pl.multiple_of((1 - b) * dsl, 128), dsl)] = yrx[0]
    else:
        out_ref[b] = final(0)
        y_copy.wait_recv()
        out_ref[1 - b] = yrx[...]

    for c in pair_kv:
        c.wait_send()
    for s in range(1, steps + 1):
        wait_send(q_sends(s), q_dn(s))
        wait_send(n_sends(s), n_up(s))
    for t in range(1, n_out):
        wait_send(up_sends(t), [w_up(t)])
        wait_send(dn_sends(t), [w_dn(t)])
    for c in [swap, y_copy] + c_copies + h_copies:
        c.wait_send()


def wide_device(queries, key_input, values, query_gain, key_gain, frames, frame_rate, out_weight):
    rows = queries.shape[0]
    hs = query_gain.shape[0]
    heads = queries.shape[1] // hs
    n = lax.axis_size("tm")
    m = lax.axis_size("head")
    n_out = n // 2
    per = rows // FRAME
    longest = n * per // 2
    back = min(WIN, longest) - 1
    reach = min((back + per - 1) // per, n - 1)
    steps = (reach + 1) // 2
    q_cnt = n_out // m
    dsl = out_weight.shape[1]

    pos = lax.axis_index("tm")
    b = pos % 2
    own_index = pos * rows + jnp.arange(rows, dtype=jnp.int32)
    cosine, sine = rotary(own_index, frames, frame_rate, hs)
    gains = jnp.stack([query_gain, key_gain])

    frames_at = jnp.arange(per, dtype=jnp.int32)
    q_pos = jnp.stack([pos + 2 * (slot // 2) for slot in range(2 * steps + 2)])
    k_pos = jnp.stack([pos, pos + 1 - 2 * b] * (steps + 1))
    q_frame = q_pos[:, None] * per + frames_at[None, :]
    q_clip = clip_of(q_frame.reshape(-1), frames)[0].reshape(q_frame.shape)
    k_frame = (k_pos[:, None] * per
               + (jnp.arange(rows, dtype=jnp.int32) // FRAME)[None, :])
    k_clip = clip_of(k_frame.reshape(-1), frames)[0].reshape(k_frame.shape)
    kf, kc = k_frame[:, None, :], k_clip[:, None, :]
    qf, qc = q_frame[:, :, None], q_clip[:, :, None]
    mask = ((kc == qc) & (kf <= qf) & (kf >= qf - (WIN - 1))).astype(jnp.float32)

    bf, f32 = jnp.bfloat16, jnp.float32
    width = heads * hs
    flat = q_cnt == 1 and dsl % 128 == 0
    shape = (rows, 2 * dsl) if flat else (2, q_cnt, rows, dsl)
    dma = pltpu.SemaphoreType.DMA
    out = pl.pallas_call(
        functools.partial(wide_kernel, (n_out, reach, steps, q_cnt, heads, hs)),
        out_shape=jax.ShapeDtypeStruct(shape, bf),
        in_specs=[pl.BlockSpec(memory_space=pl.ANY)] * 4
        + [pl.BlockSpec(memory_space=pltpu.VMEM)] * 4,
        out_specs=pl.BlockSpec(memory_space=pltpu.VMEM),
        scratch_shapes=[
            pltpu.VMEM((rows, width), bf),
            pltpu.VMEM((rows, width), bf),
            pltpu.VMEM((rows, width), bf),
            pltpu.VMEM((steps, rows, width), bf),
            pltpu.VMEM((rows, width), bf),
            pltpu.VMEM((rows, width), bf),
            pltpu.VMEM((n_out,) + out_weight.shape, bf),
            pltpu.VMEM((steps + 1, rows, width), f32),
            pltpu.VMEM((steps + 1, rows, 128), f32),
            pltpu.VMEM((steps, rows, width), bf),
            pltpu.VMEM((steps, rows, width), bf),
            pltpu.VMEM((steps, 8, rows), f32),
            pltpu.VMEM((steps, 8, rows), f32),
            pltpu.VMEM((2 * rows, width), bf),
            pltpu.VMEM((2, q_cnt, 2 * rows, dsl), bf),
            pltpu.VMEM((2, q_cnt, 2 * rows, dsl), f32),
            pltpu.VMEM((2, q_cnt, 2 * rows, dsl), bf),
            pltpu.VMEM((2, q_cnt, rows, dsl), bf),
            pltpu.VMEM((2, q_cnt, rows, dsl), bf),
            pltpu.VMEM((q_cnt, rows, dsl), bf),
            pltpu.VMEM((q_cnt, rows, dsl), bf),
            dma((steps,)), dma((steps,)), dma((2,)), dma((2,)), dma((steps, 2)), dma((steps, 2)),
            dma((n_out - 1,)), dma((n_out - 1,)), dma((n_out - 1,)), dma((n_out - 1,)),
            dma, dma, dma((2,)), dma((2,)), dma((2,)), dma((2,)), dma, dma, dma((4,)),
        ],
        compiler_params=pltpu.CompilerParams(
            collective_id=0, has_side_effects=True, vmem_limit_bytes=56 * 1024 * 1024
        ),
    )(queries, key_input, values, out_weight, cosine, sine, gains, mask)
    if flat:
        return out
    return jnp.transpose(out, (2, 1, 0, 3)).reshape(rows, 2 * q_cnt * dsl)


def level_kernel(cfg, frames_ref, rate_ref, q_hbm, k_hbm, v_hbm, w_hbm, qg_ref, kg_ref, out_ref,
                 q_in, k_in, cosine, sine, mask_ref, qtx, ktx, qx, kx, vx, num, den,
                 ntx, dtx, nrx, drx, att, far_att, wg, ptx, prx, keep, stx, xrx, ytx, yrx, rtx, rrx,
                 loc, ex_s, ex_r, qd_s, qd_r, kv_s, kv_r, nu_s, nu_r, at_s, at_r, fa_s, fa_r, r_s, r_r,
                 wu_s, wu_r, wd_s, wd_r, c_s, c_r, x_s, x_r, y_s, y_r):
    hs, mine, clips, wide_gap = cfg
    rows = q_in.shape[0]
    level = 2 * rows
    per = level // FRAME
    bf, f32, i32 = jnp.bfloat16, jnp.float32, jnp.int32
    pos = lax.axis_index("tm")
    head = lax.axis_index("head")
    z, y = pos // 2, pos % 2
    x, c = head // 2, head % 2
    partner = {"tm": pos + 1 - 2 * y}
    sibling = {"head": head + 1 - 2 * c}
    cross = {"head": lax.rem(head + 2, 4)}
    above = {"tm": pos + 2}
    below = {"tm": pos - 2}

    def lanes(i, n):
        return pl.ds(pl.multiple_of(i * n, hs), n)

    def half(i, base=0):
        return pl.ds(pl.multiple_of(base + i * rows, rows), rows)

    own_rows, other_rows = half(y), half(1 - y)

    def local(src, dst, i):
        return pltpu.make_async_copy(src, dst, loc.at[i])

    load_q = local(q_hbm, q_in, 0)
    load_k = local(k_hbm, k_in, 1)
    load_w = local(w_hbm, wg.at[z], 2)
    load_v = [local(v_hbm.at[:, lanes(mine * y + h, hs)], vx.at[h, half(y, level)], 3 + h)
              for h in range(mine)]
    for load in [load_q, load_k, load_w] + load_v:
        load.start()

    barrier = pltpu.get_barrier_semaphore()
    for near in (partner, sibling, cross):
        pl.semaphore_signal(barrier, inc=1, device_id=near, device_id_type=MESH)

    @pl.when(z < 3)
    def _():
        pl.semaphore_signal(barrier, inc=1, device_id=above, device_id_type=MESH)

    @pl.when(z > 0)
    def _():
        pl.semaphore_signal(barrier, inc=1, device_id=below, device_id_type=MESH)

    def rcopy(src, dst, s, r, where):
        return pltpu.make_async_remote_copy(
            src_ref=src, dst_ref=dst, send_sem=s, recv_sem=r,
            device_id=where, device_id_type=MESH)

    def q_ex(h):
        return rcopy(qtx.at[h], qx.at[0, h, own_rows], ex_s.at[0, h], ex_r.at[0, h], partner)

    def k_ex(h):
        return rcopy(ktx.at[h], kx.at[h, half(y, level)], ex_s.at[1, h], ex_r.at[1, h], partner)

    def v_ex(h):
        return rcopy(v_hbm.at[:, lanes(mine * (1 - y) + h, hs)], vx.at[h, half(y, level)],
                     ex_s.at[2, h], ex_r.at[2, h], partner)

    def q_dn(i, h):
        at = half(y) if i == 0 else half(1 - y)
        return rcopy(qx.at[0, h, at], qx.at[1, h, at], qd_s.at[i, h], qd_r.at[i, h], below)

    def kv_up(n, h):
        ref, i = (kx, vx)[n % 2], (y, 1 - y)[n // 2]
        return rcopy(ref.at[h, half(i, level)], ref.at[h, half(i)], kv_s.at[n, h], kv_r.at[n, h],
                     above)

    def kv_late(n, h):
        ref, first = (kx, vx)[n % 2], n // 2 == 0
        at, size = (FRAME, rows - FRAME) if first else (rows, rows)
        return rcopy(ref.at[h, pl.ds(level + at, size)], ref.at[h, pl.ds(at, size)],
                     kv_s.at[n, h], kv_r.at[n, h], above)

    def n_up(h):
        return [rcopy(ntx.at[h], nrx.at[h], nu_s.at[0, h], nu_r.at[0, h], above),
                rcopy(dtx.at[h], drx.at[h], nu_s.at[1, h], nu_r.at[1, h], above)]

    def att_dn(h):
        at = mine * y + h
        return rcopy(att.at[at], far_att.at[at], fa_s.at[0, h], fa_r.at[0, h], below)

    def far_swap(h):
        at = far_att.at[mine * y + h]
        return rcopy(at, at, fa_s.at[1, h], fa_r.at[1, h], partner)

    def r_up(j):
        return rcopy(rtx.at[j], rrx.at[j], r_s.at[j], r_r.at[j], above)

    def swap(h):
        at = att.at[mine * y + h]
        return rcopy(at, at, at_s.at[h], at_r.at[h], partner)

    def w_own(j):
        return w_hbm.at[:, pl.ds(j * hs, hs), :]

    def w_piece(o, j):
        return wg.at[o, :, pl.ds(pl.multiple_of(j * hs, hs), hs), :]

    def w_up(o, j, own=False):
        return rcopy(w_own(j) if own else w_piece(o, j), w_piece(o, j), wu_s.at[o, j], wu_r.at[o, j], above)

    def w_dn(o, j, own=False):
        return rcopy(w_own(j) if own else w_piece(o, j), w_piece(o, j), wd_s.at[o, j], wd_r.at[o, j], below)

    pieces = 3

    shape = (2 * 8, hs)
    lane = lax.broadcasted_iota(i32, shape, 1)
    sub = lax.broadcasted_iota(i32, shape, 0)
    pair = jnp.where(lane >= hs // 2, lane - hs // 2, lane)
    side = hs // 6 * 2
    depth = hs - 2 * side
    in_t = pair < depth // 2
    in_h = (pair >= depth // 2) & (pair < depth // 2 + side // 2)
    step = jnp.where(in_t, pair, jnp.where(in_h, pair - depth // 2, pair - depth // 2 - side // 2))
    log = -2.0 * math.log(10000.0)
    freq = jnp.exp(step.astype(f32) * jnp.where(in_t, log / depth, log / side))
    times = []
    for i in range(2):
        frame = 2 * pos + i
        end, start, rate = i32(0), i32(0), i32(0)
        for n in range(clips):
            inside = (frame >= end) & (frame < end + frames_ref[n])
            start = jnp.where(inside, end, start)
            rate = jnp.where(inside, rate_ref[n], rate)
            end = end + frames_ref[n]
        times.append(jnp.full(shape, frame - start, i32).astype(f32) * 24.0
                     / jnp.full(shape, rate, i32).astype(f32))
    sub8 = jnp.where(sub >= 8, sub - 8, sub)
    place = jnp.where(in_t, jnp.where(sub < 8, times[0], times[1]),
                      jnp.where(in_h, sub8, sub).astype(f32))
    angle = place * freq
    cos16 = jnp.cos(angle)
    sin16 = jnp.sin(angle) * jnp.where(lane < hs // 2, -1.0, 1.0)
    for table, small in ((cosine, cos16), (sine, sin16)):
        for i in range(2):
            for r in range(8):
                at = (8 * i + r) * GW
                table[at:at + GW, :] = jnp.where(
                    in_t, jnp.broadcast_to(small[8 * i:8 * i + 1], shape),
                    jnp.where(in_h, jnp.broadcast_to(small[r:r + 1], shape), small))

    def clip_index(frame):
        end, index = i32(0), jnp.zeros(frame.shape, i32)
        for n in range(clips):
            end = end + frames_ref[n]
            index = index + jnp.where(frame >= end, 1, 0)
        return index

    mshape = mask_ref.shape
    q_frame = per * z + lax.broadcasted_iota(i32, mshape, 0)
    k_frame = per * (z - 1) + lax.broadcasted_iota(i32, mshape, 1) // FRAME
    seen = ((clip_index(q_frame) == clip_index(k_frame)) & (k_frame <= q_frame)
            & (k_frame >= q_frame - (WIN - 1)))
    mask_ref[...] = jnp.where(seen, 1.0, 0.0)

    def rotate(src, gain_ref, i, h):
        v = src[:, lanes(mine * i + h, hs)].astype(f32)
        v = v * lax.rsqrt(jnp.mean(v * v, axis=1, keepdims=True) + 1e-06) * gain_ref[...]
        return (v * cosine[...] + pltpu.roll(v, hs // 2, 1) * sine[...]).astype(bf)

    def each(body):
        def step(h, carry):
            body(h)
            return carry
        lax.fori_loop(0, mine, step, 0)

    load_q.wait()
    load_k.wait()
    for load in load_v:
        load.wait()
    amount = 3 + (z < 3).astype(i32) + (z > 0).astype(i32)
    pl.semaphore_wait(barrier, amount)

    @pl.when((z == 2) if wide_gap else ((z == 1) | (z == 2)))
    def _():
        for j in range(2):
            w_up(z, j, True).start()

    @pl.when(z == 1)
    def _():
        for j in range(pieces):
            w_dn(1, j, True).start()

    def spread(h):
        qtx[h] = rotate(q_in, qg_ref, 1 - y, h)
        q_ex(h).start()
        qx[0, h, own_rows, :] = rotate(q_in, qg_ref, y, h)

        @pl.when((z == 3) if wide_gap else (z >= 2))
        def _():
            q_dn(0, h).start()

    def spread_keys(h):
        v_ex(h).start()
        ktx[h] = rotate(k_in, kg_ref, 1 - y, h)
        k_ex(h).start()
        kx[h, half(y, level), :] = rotate(k_in, kg_ref, y, h)

        @pl.when((z == 0) & (h == 0))
        def _():
            kv_up(0, 0).start()
            kv_up(1, 0).start()

    keys_first = z < 3 if wide_gap else z < 2

    @pl.when(keys_first)
    def _():
        each(spread_keys)

    each(spread)

    @pl.when(~keys_first)
    def _():
        each(spread_keys)

    load_w.wait()

    scale = math.log2(math.e) / math.sqrt(hs)

    def attend(h, slot, block, k0, klen, first, n=rows):
        at = pl.ds(rows * block, n)
        f0 = per * slot + (rows // FRAME) * block
        keys = slice(k0, k0 + klen)
        mask = jnp.concatenate(
            [jnp.broadcast_to(mask_ref[f0 + f:f0 + f + 1, keys], (FRAME, klen))
             for f in range(n // FRAME)], axis=0)
        ones = jnp.ones((klen, hs), bf)
        scores = lax.dot_general(qx[slot, h, at, :], kx[h, keys, :], (((1,), (1,)), ((), ())),
                                 preferred_element_type=f32)
        probs = (jnp.exp2(scores * scale) * mask).astype(bf)
        both = jnp.dot(probs, jnp.concatenate([vx[h, keys, :], ones], axis=1),
                       preferred_element_type=f32)
        if first:
            num[slot, h, at, :] = both[:, :hs]
            den[slot, h, at, :] = both[:, hs:]
        else:
            num[slot, h, at, :] += both[:, :hs]
            den[slot, h, at, :] += both[:, hs:]

    def send_sums(h):
        ntx[h] = num[1, h].astype(bf)
        dtx[h] = jnp.transpose(den[1, h])[0:8]
        for copy in n_up(h):
            copy.start()

    def add_sums(h):
        for copy in n_up(h):
            copy.wait_recv()
        num[0, h] += nrx[h].astype(f32)
        den[0, h] += jnp.transpose(jnp.concatenate([drx[h]] * (hs // 8), axis=0))

    def finish(h):
        att[mine * y + h] = (num[0, h] / den[0, h]).astype(bf)
        swap(h).start()

    def take_up(o, j):
        w_up(o, j).wait_recv()

        @pl.when(z < 3)
        def _():
            w_up(o, j).start()

    def take_dn(o, j):
        w_dn(o, j).wait_recv()

        @pl.when(z > 0)
        def _():
            w_dn(o, j).start()

    def own(h, waits=True):
        if waits:
            q_ex(h).wait_recv()
        attend(h, 0, 0, level, rows, True)
        attend(h, 0, 1, level, level, True)

    def own_below(h):
        attend(h, 0, 0, 0, level, False)
        attend(h, 0, 1, 0, level, False)

    def keys_here(h):
        k_ex(h).wait_recv()
        v_ex(h).wait_recv()

    def queries_here(h):
        q_dn(0, h).wait_recv()
        q_dn(1, h).wait_recv()

    def queries_down():
        for h in range(mine):
            q_ex(h).wait_recv()
            q_dn(1, h).start()

    def take_far():
        for h in range(mine):
            if h == 2:
                take_dn(3, 2)
            att_dn(h).wait_recv()
            far_swap(h).start()

    @pl.when(z == 0)
    def _():
        for h in range(mine):
            if h + 1 < mine:
                kv_up(0, h + 1).start()
                kv_up(1, h + 1).start()
            k_ex(h).wait_recv()
            kv_up(2, h).start()
            v_ex(h).wait_recv()
            kv_up(3, h).start()
        for j in range(pieces):
            w_up(0, j, True).start()

        def rest(h):
            own(h)
            finish(h)

        each(rest)

    @pl.when(z == 1)
    def _():
        if wide_gap:
            for i in range(2):
                @pl.when(y == i)
                def _():
                    for h in range(mine):
                        kv_late(2 * i, h).start()
                        kv_late(2 * i + 1, h).start()
            for h in range(mine):
                for n, copy in ((0, k_ex), (1, v_ex)):
                    copy(h).wait_recv()
                    for i in range(2):
                        @pl.when(y != i)
                        def _():
                            kv_late(2 * i + n, h).start()
            for j in range(pieces):
                w_up(1, j, True).start()
            for j in range(2):
                take_dn(2, j)
            each(own)
        else:
            for h in range(mine):
                keys_here(h)
                queries_here(h)
                attend(h, 1, 0, level, level, True)
                attend(h, 1, 1, level, level, True)
                for n in range(4):
                    kv_up(n, h).wait_recv()
                attend(h, 1, 0, 0, level, False)
                attend(h, 1, 1, rows, rows, False)
                send_sums(h)
                if h == 0:
                    w_up(1, 2, True).start()
                else:
                    take_dn(2, h - 1)
            each(own)

        def rest(h):
            if wide_gap:
                for n in range(4):
                    kv_up(n, h).wait_recv()
            own_below(h)
            finish(h)

        take_dn(2, 2)
        each(rest)
        take_up(0, 0)
        take_dn(3, 0)
        take_up(0, 1)

    @pl.when(z == 2)
    def _():
        if not wide_gap:
            queries_down()
        for j in range(pieces):
            w_dn(2, j, True).start()

        def above_sums(h):
            keys_here(h)
            queries_here(h)
            attend(h, 1, 0, level, level, True)
            attend(h, 1, 1, level, level, True)
            if wide_gap:
                for n in range(4):
                    kv_late(n, h).wait_recv()
                attend(h, 1, 0, FRAME, level - FRAME, False)
                attend(h, 1, 1, rows, rows, False)
            send_sums(h)

        def rest(h):
            if wide_gap:
                own(h)
                attend(h, 0, 0, FRAME, level - FRAME, False)
                attend(h, 0, 1, FRAME, level - FRAME, False)
            else:
                add_sums(h)
            finish(h)

        each(above_sums)
        w_up(2, 2, True).start()
        if not wide_gap:
            for j in range(2):
                take_up(1, j)
            each(lambda h: own(h, False))
        for j in range(2):
            take_dn(3, j)
        each(rest)
        if not wide_gap:
            take_far()

    @pl.when(z == 3)
    def _():
        queries_down()
        for j in range(2):
            w_dn(3, j, True).start()

        def here(h):
            keys_here(h)
            own(h, False)

        def last(h):
            add_sums(h)
            finish(h)
            att_dn(h).start()

        each(here)
        for h in range(mine):
            if h == 2:
                w_dn(3, 2, True).start()
            last(h)

    for h in range(mine):
        swap(h).wait_recv()

    def order(n):
        t, j = n // pieces, n % pieces
        from_one = jnp.where(t == 0, 1, jnp.where(t == 1, 2, jnp.where(t == 2, 0, 3)))
        low = jnp.where((z == 1) | (z == 2), from_one, t)
        o = jnp.where(z < 2, low, 3 - low)
        both = (z == 2) & (n >= 2 * pieces)
        late = n - 2 * pieces
        extra = both & (late % 3 == 0)
        o = jnp.where(both, jnp.where(late % 3 == 1, 3, 0), o)
        j = jnp.where(both, late // 3, j)
        return o, j, extra

    count = jnp.where(z == 2, 5 * pieces, jnp.where(z == 3, 3 * pieces, 4 * pieces))

    def sum_at(o, j, extra):
        return jnp.where(extra, 2 * pieces, (o // 2) * pieces) + j

    def to_sibling(m):
        return rcopy(ptx.at[m], prx.at[m], c_s.at[m], c_r.at[m], sibling)

    def to_cross(i):
        return rcopy(stx.at[i], xrx.at[i], x_s.at[i], x_r.at[i], cross)

    def to_partner(j):
        return rcopy(ytx.at[j], yrx.at[j], y_s.at[j], y_r.at[j], partner)

    def result(j):
        m = (head // 2) * pieces + j
        to_cross(j).wait_recv()
        ytx[j] = (keep[m, other_rows, :] + xrx[j, other_rows, :].astype(f32)).astype(bf)
        to_partner(j).start()
        out_ref[:, lanes(pieces * y + j, hs)] = (
            keep[m, own_rows, :] + xrx[j, own_rows, :].astype(f32)).astype(bf)

    def far_sum(j):
        r_up(j).wait_recv()

        @pl.when(x == 0)
        def _():
            keep[j] = rrx[j].astype(f32)

        @pl.when(x == 1)
        def _():
            stx[j] = rrx[j]
            to_cross(j).start()

    lag = jnp.where(z == 0, 1, jnp.where(z == 2, 2, 3))

    def project(n, carry):
        o1, j1, extra1 = order(n - lag)

        @pl.when((n >= lag) & (n < count + lag) & (o1 % 2 == c))
        def _():
            m = sum_at(o1, j1, extra1)
            to_sibling(m).wait_recv()

            @pl.when(extra1)
            def _():
                rtx[j1] = (keep[m] + prx[m].astype(f32)).astype(bf)
                r_up(j1).start()

            @pl.when(~extra1 & (o1 // 2 != x))
            def _():
                stx[j1] = (keep[m] + prx[m].astype(f32)).astype(bf)
                to_cross(j1).start()

            @pl.when(~extra1 & (o1 // 2 == x))
            def _():
                keep[m] = keep[m] + prx[m].astype(f32)

        @pl.when((z == 1) & (n == 2))
        def _():
            take_up(0, 2)

        @pl.when((z == 1) & (n == 1))
        def _():
            take_dn(3, 1)

        @pl.when((z == 1) & (n == 6))
        def _():
            take_dn(3, 2)

        if wide_gap:
            @pl.when((z == 2) & (n < pieces))
            def _():
                take_up(1, n)
        else:
            @pl.when((z == 2) & (n == 0))
            def _():
                take_up(1, 2)

        if wide_gap:
            @pl.when((z == 2) & (n == 0))
            def _():
                take_far()

        @pl.when((z == 2) & (n == 2 * pieces))
        def _():
            for h in range(mine):
                far_swap(h).wait_recv()

        @pl.when(n < count)
        def _():
            o, j, extra = order(n)

            @pl.when((z == 0) & (o > 0))
            def _():
                w_dn(o, j).wait_recv()

            @pl.when((z == 3) & (o < 3))
            def _():
                w_up(o, j).wait_recv()

            @pl.when(extra)
            def _():
                w_up(0, j).wait_recv()

            weight = jnp.concatenate(
                [wg[o, h, pl.ds(pl.multiple_of(j * hs, hs), hs), :] for h in range(2 * mine)], axis=1)
            m = sum_at(o, j, extra)

            def spread_sum(held):
                rows_in = jnp.concatenate([held[h] for h in range(2 * mine)], axis=1)
                acc = lax.dot_general(rows_in, weight, (((1,), (1,)), ((), ())),
                                      preferred_element_type=f32)

                @pl.when(o % 2 != c)
                def _():
                    ptx[m] = acc.astype(bf)
                    to_sibling(m).start()

                @pl.when(o % 2 == c)
                def _():
                    keep[m] = acc

            @pl.when(extra)
            def _():
                spread_sum(far_att)

            @pl.when(~extra)
            def _():
                spread_sum(att)

        return carry

    lax.fori_loop(0, count + lag, project, 0)

    bare = (z == 3) & (head == 0)

    @pl.when(~bare)
    def _():
        for j in range(pieces):
            result(j)

    @pl.when((z == 3) & (c == 0))
    def _():
        for j in range(pieces):
            far_sum(j)

    @pl.when(bare)
    def _():
        for j in range(pieces):
            result(j)

    for j in range(pieces):
        to_partner(j).wait_recv()
        out_ref[:, lanes(pieces * (1 - y) + j, hs)] = yrx[j]

    def sent(h):
        for copy in (q_ex(h), k_ex(h), v_ex(h), swap(h)):
            copy.wait_send()

        @pl.when((z == 3) if wide_gap else (z >= 2))
        def _():
            q_dn(0, h).wait_send()
            q_dn(1, h).wait_send()

        @pl.when(z == 0)
        def _():
            for n in range(4):
                kv_up(n, h).wait_send()

        @pl.when((z == 2) if wide_gap else ((z == 1) | (z == 2)))
        def _():
            for copy in n_up(h):
                copy.wait_send()

        if wide_gap:
            @pl.when(z == 1)
            def _():
                for n in range(4):
                    kv_late(n, h).wait_send()

        @pl.when(z == 3)
        def _():
            att_dn(h).wait_send()

        @pl.when(z == 2)
        def _():
            far_swap(h).wait_send()

    each(sent)

    for o in range(4):
        @pl.when(((z == 0) | (z == 1)) if o == 0 else ((z < 3) & (z >= o)))
        def _():
            for j in range(pieces):
                w_up(o, j).wait_send()

        @pl.when((z > 0) & (z <= o))
        def _():
            for j in range(pieces):
                w_dn(o, j).wait_send()

    @pl.when(~((z == 3) & (c == 1)))
    def _():
        for m in range(pieces):
            to_sibling(m).wait_send()
    for m in range(pieces, 2 * pieces):
        to_sibling(m).wait_send()

    @pl.when((z == 2) & (c == 1))
    def _():
        for m in range(2 * pieces, 3 * pieces):
            to_sibling(m).wait_send()

    @pl.when((z == 2) & (c == 0))
    def _():
        for j in range(pieces):
            r_up(j).wait_send()
    for j in range(pieces):
        to_cross(j).wait_send()
        to_partner(j).wait_send()


def level_device(wide_gap, queries, key_input, values, query_gain, key_gain, frames, frame_rate, out_weight):
    rows, width = queries.shape
    hs = query_gain.shape[0]
    mine = width // hs // 2
    level = 2 * rows
    pieces = out_weight.shape[1] // hs
    bf, f32 = jnp.bfloat16, jnp.float32
    dma = pltpu.SemaphoreType.DMA
    vmem = pltpu.VMEM
    smem = pl.BlockSpec(memory_space=pltpu.SMEM)
    near = pl.BlockSpec(memory_space=pltpu.VMEM)
    far = pl.BlockSpec(memory_space=pl.ANY)
    return pl.pallas_call(
        functools.partial(level_kernel, (hs, mine, frames.shape[0], wide_gap)),
        out_shape=jax.ShapeDtypeStruct((rows, width), bf),
        in_specs=[smem, smem, far, far, far, far, near, near],
        out_specs=near,
        scratch_shapes=[
            vmem((rows, width), bf), vmem((rows, width), bf),
            vmem((rows, hs), f32), vmem((rows, hs), f32),
            vmem((16, 2 * level), f32),
            vmem((mine, rows, hs), bf), vmem((mine, rows, hs), bf),
            vmem((2, mine, level, hs), bf),
            vmem((mine, 2 * level, hs), bf), vmem((mine, 2 * level, hs), bf),
            vmem((2, mine, level, hs), f32), vmem((2, mine, level, hs), f32),
            vmem((mine, level, hs), bf), vmem((mine, 8, level), f32),
            vmem((mine, level, hs), bf), vmem((mine, 8, level), f32),
            vmem((2 * mine, level, hs), bf), vmem((2 * mine, level, hs), bf),
            vmem((4,) + out_weight.shape, bf),
            vmem((3 * pieces, level, hs), bf), vmem((3 * pieces, level, hs), bf),
            vmem((3 * pieces, level, hs), f32),
            vmem((pieces, level, hs), bf), vmem((pieces, level, hs), bf),
            vmem((pieces, rows, hs), bf), vmem((pieces, rows, hs), bf),
            vmem((pieces, level, hs), bf), vmem((pieces, level, hs), bf),
            dma((3 + mine,)), dma((3, mine)), dma((3, mine)), dma((2, mine)), dma((2, mine)),
            dma((4, mine)), dma((4, mine)), dma((2, mine)), dma((2, mine)),
            dma((mine,)), dma((mine,)), dma((2, mine)), dma((2, mine)), dma((pieces,)), dma((pieces,)),
            dma((4, pieces)), dma((4, pieces)), dma((4, pieces)), dma((4, pieces)),
            dma((3 * pieces,)), dma((3 * pieces,)), dma((pieces,)), dma((pieces,)),
            dma((pieces,)), dma((pieces,)),
        ],
        compiler_params=pltpu.CompilerParams(
            collective_id=int(wide_gap), has_side_effects=True, vmem_limit_bytes=56 * 1024 * 1024
        ),
    )(frames, frame_rate, queries, key_input, values, out_weight,
      query_gain.reshape(1, hs), key_gain.reshape(1, hs))


def per_device(queries, key_input, values, query_gain, key_gain, frames, frame_rate, out_weight):
    args = (queries, key_input, values, query_gain, key_gain, frames, frame_rate, out_weight)
    rows, width = queries.shape
    heads, columns, hs = out_weight.shape
    fits = (lax.axis_size("tm") == 8 and lax.axis_size("head") == 4 and rows == 2 * FRAME
            and FRAME == 8 * GW and hs == 128 and heads % 2 == 0
            and columns == width // 2 == 3 * hs)
    if fits:
        count = frames.shape[0]
        upto = jnp.arange(count)[:, None] >= jnp.arange(count)[None, :]
        ends = jnp.sum(jnp.where(upto, frames[None, :], 0), axis=1)
        spans = (ends - frames <= 7) & (ends > 12)
        return lax.cond(jnp.any(spans), functools.partial(level_device, True),
                        functools.partial(level_device, False), *args)
    return wide_device(*args)


def solution(mesh):
    in_specs = (
        P("tm", "head"),
        P("tm", "head"),
        P("tm", "head"),
        P(),
        P(),
        P(),
        P(),
        P("head", "tm", None),
    )
    out_specs = P("tm", "head")
    return jax.shard_map(
        per_device, mesh=mesh, in_specs=in_specs, out_specs=out_specs, check_vma=False
    )
```
